32 devices in a mesh: groups: 2 (over x), band: 16 (over z, y, core).
Axes of the slice: x: 2, y: 2, z: 4, core: 2. Of those that a mesh axis runs over, the one named last changes fastest.
Arguments:
- grid_feats: bfloat16 [32768, 600], P(('groups', 'band')), parts along dimension 0, may hold values from -6 to 6
- mesh_embed: bfloat16 [4096, 256], P(('groups', 'band')), parts along dimension 0, may hold values from -6 to 6
- edge_latent: bfloat16 [32768, 256], P(('groups', 'band')), parts along dimension 0, may hold values from -3 to 3
- grid_node: int32 [16384], P('band'), may hold values from 0 to 2047, as said below
- fetch_table: int32 [16, 16, 16], P('band'), may hold values from 0 to 127
- edge_sender: int32 [16384], P('band'), may hold values from 0 to 255
- edge_receiver: int32 [16384], P('band'), may hold values from 0 to 127
- block_count: int32 [16], P('band'), may hold values from 1 to 8, as said below
- w_grid: bfloat16 [600, 256], replicated, may hold values from -0.25 to 0.25
- enc_w1: bfloat16 [256, 256], replicated, may hold values from -0.375 to 0.375
- enc_w2: bfloat16 [256, 256], replicated, may hold values from -0.375 to 0.375
- edge_w1: bfloat16 [4, 768, 256], replicated, may hold values from -1 to 1
- edge_w2: bfloat16 [4, 256, 256], replicated, may hold values from -0.375 to 0.375
- node_w1: bfloat16 [4, 512, 256], replicated, may hold values from -1 to 1
- node_w2: bfloat16 [4, 256, 256], replicated, may hold values from -1 to 1
Outputs:
- nodes: bfloat16 [4096, 256], P(('groups', 'band')), parts along dimension 0
The draws below stay inside these ranges and needn't reach their ends.
There are 2 independent parts, one for each index of `groups`. The reference program is written for one: setup_inputs(seed, part) draws one part's arguments, and reference() takes and returns one part's arrays. A program takes and returns all parts, laid end to end along the dimension named above; an argument that names none is the same for every part. Nothing has to cross between parts.
Inputs may be any that keep to these rules, and one draw needn't show every extreme that they name: `grid_node`: A grid point of band b, that is of rows b * 1024 onward, feeds a node of owner b - 1, b or b + 1 (node o * 128 + r has owner o). `block_count`: some owner has exactly 8 live blocks.
All inputs are finite; a program needn't handle non-finite values.
Results may differ from the reference program's by a relative error of at most 0.017.
Values may be sent and summed in bfloat16 or wider, within the bound.
A program may use at most 64 MiB of HBM per device.

```python
import jax
import jax.numpy as jnp
from jax import lax

H = 256
CG = 600
M_DEV = 128
G_DEV = 1024
CAP = 16
EDGE_BLOCK = 128
EB_MAX = 8
LAYERS = 4
OWNERS = 16
NODES = 2048
GRID = 16384
EDGES = 16384
SLOTS = 256


def orthogonal(key, layers, width):
    drawn = jax.random.normal(key, (layers, width, width), jnp.float32)
    basis, upper = jnp.linalg.qr(drawn)
    diagonal = jnp.diagonal(upper, axis1=-2, axis2=-1)
    flips = jnp.where(diagonal >= 0.0, jnp.float32(1.0), jnp.float32(-1.0))
    return basis * flips[:, None, :]


def draw_grid_node(key, part):
    first, second = jax.random.split(jax.random.fold_in(key, 11), 2)
    owners = GRID // G_DEV
    band = jnp.arange(GRID, dtype=jnp.int32) // G_DEV
    pick = jax.random.randint(first, (GRID,), 0, 8)
    offset = jnp.where(pick == 0, -1, jnp.where(pick == 1, 1, 0))
    owner = jnp.clip(band + offset, 0, owners - 1)
    local = jax.random.randint(second, (GRID,), 0, M_DEV)
    return (owner * M_DEV + local).astype(jnp.int32)


def draw_block_count(key, part):
    first, second = jax.random.split(jax.random.fold_in(key, 23), 2)
    owners = NODES // M_DEV
    counts = jax.random.randint(first, (owners,), 1, max(2, EB_MAX // 2) + 1)
    chosen = jax.random.randint(second, (), 0, owners)
    counts = jnp.where(jnp.arange(owners) == chosen, EB_MAX, counts)
    return counts.astype(jnp.int32)


def draw_edge_w1(key, part):
    first, second, third = jax.random.split(jax.random.fold_in(key, 31), 3)
    edge_part = 0.3 * orthogonal(first, LAYERS, H)
    sender_part = 1.0 * orthogonal(second, LAYERS, H)
    receiver_part = 0.3 * orthogonal(third, LAYERS, H)
    return jnp.concatenate([edge_part, sender_part, receiver_part], axis=1).astype(jnp.bfloat16)


def draw_node_w1(key, part):
    first, second = jax.random.split(jax.random.fold_in(key, 37), 2)
    node_part = 0.5 * orthogonal(first, LAYERS, H)
    summed_part = 1.0 * orthogonal(second, LAYERS, H)
    return jnp.concatenate([node_part, summed_part], axis=1).astype(jnp.bfloat16)


def draw_node_w2(key, part):
    return orthogonal(jax.random.fold_in(key, 41), LAYERS, H).astype(jnp.bfloat16)


def touch_ends(result, rng, least, top_value):
    shape = result.shape
    spot = [jax.random.randint(jax.random.fold_in(rng, axis), (), 0, shape[axis]) for axis in range(len(shape))]
    result = result.at[tuple(spot)].set(least)
    longest = shape.index(max(shape))
    spot[longest] = (spot[longest] + 1) % shape[longest]
    return result.at[tuple(spot)].set(top_value)


def steps_of(own_key, shape, cuts, smallest, largest):
    factor_of = 1.0
    for position, shards_of in cuts:
        heights = jax.random.uniform(jax.random.fold_in(jax.random.fold_in(own_key, 6), position), (shards_of,), jnp.float32, smallest / len(cuts), largest / len(cuts))
        factor_of = factor_of * jnp.repeat(jnp.exp(heights), shape[position] // shards_of).reshape((-1,) + (1,) * (len(shape) - 1 - position))
    return factor_of


def scatter_about(stream_key, shape, spread, reach, cuts=(), kind=jnp.bfloat16):
    array = jax.random.normal(stream_key, shape, jnp.float32) * spread
    if len(cuts) > 0:
        array = steps_of(stream_key, shape, cuts, -0.22, 0.18) * array
    return jnp.clip(array, min=-reach, max=reach).astype(kind)


def setup_inputs(seed: int = 0, part: int = 0) -> dict:
    splits = jax.random.split(jax.random.key(seed), 16)
    part_keys = jax.random.split(jax.random.fold_in(splits[15], part), 16)
    grid_feats = scatter_about(part_keys[0], (GRID, CG), 1.0, 6.0, ((0, 16),))
    mesh_embed = scatter_about(part_keys[1], (NODES, H), 1.0, 6.0, ((0, 16),))
    edge_latent = scatter_about(part_keys[2], (EDGES, H), 0.5, 3.0, ((0, 16),))
    grid_node = draw_grid_node(jax.random.fold_in(splits[15], 71), part)
    fetch_table = touch_ends(jax.random.randint(splits[4], (OWNERS, OWNERS, CAP), 0, M_DEV), jax.random.fold_in(splits[4], 1), 0, M_DEV - 1).astype(jnp.int32)
    edge_sender = touch_ends(jax.random.randint(splits[5], (EDGES,), 0, SLOTS), jax.random.fold_in(splits[5], 1), 0, SLOTS - 1).astype(jnp.int32)
    edge_receiver = touch_ends(jax.random.randint(splits[6], (EDGES,), 0, M_DEV), jax.random.fold_in(splits[6], 1), 0, M_DEV - 1).astype(jnp.int32)
    block_count = draw_block_count(jax.random.fold_in(splits[15], 71), part)
    w_grid = scatter_about(splits[8], (CG, H), CG ** -0.5, 0.25)
    enc_w1 = scatter_about(splits[9], (H, H), H ** -0.5, 0.375)
    enc_w2 = scatter_about(splits[10], (H, H), H ** -0.5, 0.375)
    edge_w1 = draw_edge_w1(jax.random.fold_in(splits[15], 71), part)
    edge_w2 = scatter_about(splits[12], (LAYERS, H, H), H ** -0.5, 0.375)
    node_w1 = draw_node_w1(jax.random.fold_in(splits[15], 71), part)
    node_w2 = draw_node_w2(jax.random.fold_in(splits[15], 71), part)
    return {"grid_feats": grid_feats, "mesh_embed": mesh_embed, "edge_latent": edge_latent, "grid_node": grid_node, "fetch_table": fetch_table, "edge_sender": edge_sender, "edge_receiver": edge_receiver, "block_count": block_count, "w_grid": w_grid, "enc_w1": enc_w1, "enc_w2": enc_w2, "edge_w1": edge_w1, "edge_w2": edge_w2, "node_w1": node_w1, "node_w2": node_w2}


def norm(value):
    mean = lax.optimization_barrier(jnp.mean(value, axis=-1, keepdims=True))
    centered = value - mean
    var = lax.optimization_barrier(jnp.mean(centered * centered, axis=-1, keepdims=True))
    return centered / jnp.sqrt(var + 1e-05)

def mlp(inputs, first, second):
    hidden = jax.nn.silu(jnp.dot(inputs.astype(jnp.float32), first.astype(jnp.float32), preferred_element_type=jnp.float32)).astype(jnp.bfloat16)
    return norm(jnp.dot(hidden.astype(jnp.float32), second.astype(jnp.float32), preferred_element_type=jnp.float32))

def reference(grid_feats, mesh_embed, edge_latent, grid_node, fetch_table, edge_sender, edge_receiver, block_count, w_grid, enc_w1, enc_w2, edge_w1, edge_w2, node_w1, node_w2):
    latent = jax.nn.silu(jnp.dot(grid_feats.astype(jnp.float32), w_grid.astype(jnp.float32), preferred_element_type=jnp.float32)).astype(jnp.bfloat16)
    agg = jax.ops.segment_sum(latent.astype(jnp.float32), grid_node, num_segments=NODES)
    nodes = (mesh_embed.astype(jnp.float32) + mlp(agg.astype(jnp.bfloat16), enc_w1, enc_w2)).astype(jnp.bfloat16)
    per_owner = EB_MAX * EDGE_BLOCK
    rows = jnp.arange(EDGES, dtype=jnp.int32)
    owner = (rows // per_owner).astype(jnp.int32)
    slot_owner = (edge_sender // CAP).astype(jnp.int32)
    slot_col = (edge_sender % CAP).astype(jnp.int32)
    sender = (slot_owner * M_DEV + fetch_table[owner, slot_owner, slot_col]).astype(jnp.int32)
    receiver = (owner * M_DEV + edge_receiver).astype(jnp.int32)
    live = rows % per_owner < block_count[owner] * EDGE_BLOCK
    for layer in range(LAYERS):
        joined = jnp.concatenate([edge_latent, nodes[sender], nodes[receiver]], axis=1)
        message = mlp(joined, edge_w1[layer], edge_w2[layer])
        edge_latent = (edge_latent.astype(jnp.float32) + message).astype(jnp.bfloat16)
        masked = jnp.where(live[:, None], edge_latent.astype(jnp.float32), jnp.float32(0.0))
        summed = jax.ops.segment_sum(masked, receiver, num_segments=NODES)
        joined_nodes = jnp.concatenate([nodes, summed.astype(jnp.bfloat16)], axis=1)
        update = mlp(joined_nodes, node_w1[layer], node_w2[layer])
        nodes = (nodes.astype(jnp.float32) + update).astype(jnp.bfloat16)
    return nodes
```

```python
import functools

import jax
import jax.numpy as jnp
from jax import lax
from jax.experimental import pallas as pl
from jax.experimental.pallas import tpu as pltpu
from jax.sharding import PartitionSpec as P

EDGE_BLOCK = 128
LANES = 128
ROWS = 256
CHUNK = 1024
F32 = jnp.float32
BF16 = jnp.bfloat16


def silu_of_half(half):
    return half + half * jnp.tanh(half)


def silu(value):
    return silu_of_half(value * 0.5)


def center(weight):
    value = weight.astype(F32)
    return (value - jnp.mean(value, axis=-1, keepdims=True)).astype(BF16)


def inverse_scale(value):
    var = jnp.sum(value * value, axis=-1, keepdims=True) * (1.0 / value.shape[-1])
    return lax.rsqrt(var + 1e-05)


def dot(left, right):
    return jnp.dot(left, right, preferred_element_type=F32)


def peer_order(me, n):
    if n & (n - 1):
        return [lax.rem(me + step, n) for step in range(1, n)]
    peers = [0]
    place = 1
    while place < n:
        bit = lax.rem(lax.div(me, place), 2)
        same, other = bit * place, (1 - bit) * place
        peers = [low + same for low in peers] + [low + other for low in peers]
        place *= 2
    return peers[:0:-1]


def slot_of(owner, me, n):
    if n & (n - 1):
        return lax.rem(owner - me + 2 * n - 1, n)
    return (n - 1) - lax.bitwise_xor(owner, jnp.full(owner.shape, me, jnp.int32))


def kernel(
    n,
    grid_feats,
    mesh_embed,
    edge_latent,
    grid_node,
    fetch_table,
    edge_sender,
    edge_receiver,
    block_count,
    w_grid,
    enc_w1,
    enc_w2,
    edge_w1,
    edge_w2,
    node_w1,
    node_w2,
    out,
    gf,
    wg,
    wg_t,
    me_v,
    ew1,
    ew2,
    e1,
    e2,
    n1,
    n2,
    edges,
    gn,
    table,
    es,
    er,
    count,
    grid_hot,
    latent,
    part_send,
    part_recv,
    table_send,
    table_recv,
    pick,
    pick_sum,
    send_hot,
    recv_hot,
    recv_hot_t,
    local,
    message,
    nodes_ref,
    picked,
    picked_base,
    picked_part,
    picked_sent,
    mixed,
    outgoing,
    incoming,
    load_sem,
    part_send_sem,
    part_recv_sem,
    table_send_sem,
    table_recv_sem,
    send_sem,
    recv_sem,
):
    me = lax.axis_index("band")
    nodes_dev, width = mesh_embed.shape
    layers = edge_w1.shape[0]
    cap = fetch_table.shape[2]
    edge_rows = edge_latent.shape[0]
    grid_rows = grid_feats.shape[1]

    peers = peer_order(me, n)
    barrier = pltpu.get_barrier_semaphore()
    for peer in peers:
        pl.semaphore_signal(barrier, inc=1, device_id={"band": peer})

    pairs = [
        (grid_node, gn),
        (w_grid, wg),
        (grid_feats, gf),
        (fetch_table.at[0], table),
        (edge_sender, es),
        (edge_receiver, er),
        (block_count, count),
        (mesh_embed, me_v),
        (enc_w1, ew1),
        (enc_w2, ew2),
        (edge_w1, e1),
        (edge_latent, edges),
        (node_w2, n2),
        (edge_w2, e2),
        (node_w1, n1),
    ]
    loads = [
        pltpu.make_async_copy(source, target, load_sem.at[index])
        for index, (source, target) in enumerate(pairs)
    ]
    for load in loads[:7]:
        load.start()

    loads[0].wait()
    first = (me - 1) * nodes_dev
    for row in range(grid_rows // LANES):
        column = gn[row : row + 1, :] - first
        hot = lax.broadcasted_iota(jnp.int32, (3 * nodes_dev, LANES), 0) == column
        grid_hot[:, row * LANES : (row + 1) * LANES] = hot.astype(F32).astype(BF16)
    loads[3].wait()
    for owner in range(n):
        table_send[owner, :, :cap] = table[owner : owner + 1, :]
    table_recv[n - 1] = table_send[me]
    loads[1].wait()
    wg_t[...] = wg[...].T
    loads[2].wait()
    for load in loads[7:]:
        load.start()
    for start in range(0, grid_rows, ROWS):
        rows = slice(start, start + ROWS)
        latent[:, rows] = silu(dot(wg_t[...], gf[:, rows])).astype(BF16)
    partial = lax.dot_general(
        grid_hot[...], latent[...], (((1,), (1,)), ((), ())), preferred_element_type=F32
    )
    part_send[0] = partial[:nodes_dev].astype(BF16)
    part_send[1] = partial[2 * nodes_dev :].astype(BF16)
    own = partial[nodes_dev : 2 * nodes_dev]

    pl.semaphore_wait(barrier, n - 1)

    def part_copy(slot, target):
        return pltpu.make_async_remote_copy(
            src_ref=part_send.at[slot],
            dst_ref=part_recv.at[slot],
            send_sem=part_send_sem.at[slot],
            recv_sem=part_recv_sem.at[slot],
            device_id={"band": target},
        )

    below = lax.rem(me + n - 1, n)
    above = lax.rem(me + 1, n)
    down = part_copy(0, below)
    up = part_copy(1, above)

    def table_copy(slot, peer):
        return pltpu.make_async_remote_copy(
            src_ref=table_send.at[peer],
            dst_ref=table_recv.at[slot],
            send_sem=table_send_sem,
            recv_sem=table_recv_sem,
            device_id={"band": peer},
        )

    half = n // 2
    for slot in range(half):
        table_copy(slot, peers[slot]).start()

    @pl.when(me > 0)
    def _():
        down.start()

    @pl.when(me < n - 1)
    def _():
        up.start()

    for slot in range(half, n - 1):
        table_copy(slot, peers[slot]).start()

    loads[4].wait()
    loads[5].wait()
    loads[6].wait()
    live_rows = count[0] * EDGE_BLOCK
    slots = es[...]
    owner = lax.div(slots, cap)
    slots = slot_of(owner, me, n) * cap + (slots - owner * cap)
    for row in range(edge_rows // LANES):
        rows = slice(row * LANES, (row + 1) * LANES)
        lane = lax.broadcasted_iota(jnp.int32, (LANES, LANES), 1)
        sender = jnp.broadcast_to(slots[row : row + 1, :], (LANES, LANES)).T
        for base in range(0, n * cap, LANES):
            hot = (sender == lane + base).astype(F32).astype(BF16)
            send_hot[rows, base : base + LANES] = hot
        value = er[row : row + 1, :]
        receiver = jnp.broadcast_to(value, (LANES, LANES)).T
        for base in range(0, nodes_dev, LANES):
            hot = (receiver == lane + base).astype(F32).astype(BF16)
            recv_hot[rows, base : base + LANES] = hot
        place = lax.broadcasted_iota(jnp.int32, (1, LANES), 1) + row * LANES
        masked = jnp.where(place < live_rows, value, -1)
        hot = lax.broadcasted_iota(jnp.int32, (nodes_dev, LANES), 0) == masked
        recv_hot_t[:, rows] = hot.astype(F32).astype(BF16)

    def sender_weight(layer):
        return e1[layer, width : 2 * width, :]

    for index in range(7, 15):
        loads[index].wait()
    ew2[...] = center(ew2[...])
    mixed[layers - 1] = dot(ew2[...], sender_weight(0)).astype(BF16)
    embed_sent = dot(me_v[...], sender_weight(0)) * 0.5
    for layer in range(layers):
        e2[layer] = center(e2[layer])
        n2[layer] = center(n2[layer])
    for layer in range(layers - 1):
        mixed[layer] = dot(n2[layer], sender_weight(layer + 1)).astype(BF16)

    @pl.when(me > 0)
    def _():
        part_copy(1, above).wait_recv()

    @pl.when(me == 0)
    def _():
        part_recv[1] = jnp.zeros((nodes_dev, width), BF16)

    @pl.when(me < n - 1)
    def _():
        part_copy(0, below).wait_recv()

    @pl.when(me == n - 1)
    def _():
        part_recv[0] = jnp.zeros((nodes_dev, width), BF16)

    agg = own + part_recv[0].astype(F32) + part_recv[1].astype(F32)
    hidden = silu(dot(agg.astype(BF16), ew1[...])).astype(BF16)
    update = dot(hidden, ew2[...])
    turned = dot(hidden, mixed[layers - 1])
    scale = inverse_scale(update)
    sent = (embed_sent + (0.5 * scale) * turned).astype(BF16)
    nodes_ref[...] = (me_v[...].astype(F32) + scale * update).astype(BF16)

    def several(refs, sems):
        return pltpu.make_async_copy(refs, refs, sems)

    several(table_recv.at[pl.ds(0, n - 1)], table_recv_sem).wait()
    wanted = jnp.broadcast_to(table_recv[...], (n, cap, LANES)).reshape(n * cap, LANES)
    slot = lax.rem(lax.broadcasted_iota(jnp.int32, (n * cap, LANES), 0), cap)
    lane = lax.broadcasted_iota(jnp.int32, (n * cap, LANES), 1)
    column = jnp.sum(jnp.where(slot == lane, wanted, 0).astype(F32), axis=1, keepdims=True)
    lane = lax.broadcasted_iota(jnp.int32, (n * cap, nodes_dev), 1).astype(F32)
    pick[...] = (column == lane).astype(F32).astype(BF16)

    def layer_copy(layer, slot, peer):
        return pltpu.make_async_remote_copy(
            src_ref=outgoing.at[slot],
            dst_ref=incoming.at[lax.rem(layer, 2), slot],
            send_sem=send_sem,
            recv_sem=recv_sem.at[lax.rem(layer, 2)],
            device_id={"band": peer},
        )

    def send(layer):
        for slot, peer in enumerate(peers):
            layer_copy(layer, slot, peer).start()
        incoming[lax.rem(layer, 2), n - 1] = outgoing[n - 1]

    def prepare(layer):
        nodes = nodes_ref[...]
        kept = dot(nodes, e1[layer, 2 * width :, :]).astype(BF16)
        for start in range(0, edge_rows, ROWS):
            rows = slice(start, start + ROWS)
            joined = dot(edges[rows, :], e1[layer, :width, :]) + dot(recv_hot[rows, :], kept)
            local[rows, :] = joined * 0.5

    def prepare_picked(layer):
        picked_base[...] = dot(pick_sum[...], edges[...])
        picked_part[...] = dot(picked[...], n1[layer, :width, :])
        picked_sent[...] = dot(picked[...], sender_weight(layer + 1)) * 0.5

    def arrivals(layer):
        parity = lax.rem(layer, 2)
        several(incoming.at[parity, pl.ds(0, n - 1)], recv_sem.at[parity]).wait()
        several(outgoing.at[pl.ds(0, n - 1)], send_sem).wait()
        senders = incoming[parity].reshape(n * cap, width)
        for start in range(0, edge_rows, CHUNK):
            rows = slice(start, start + CHUNK)
            before = local[rows, :] + dot(send_hot[rows, :], senders)
            hidden = silu_of_half(before.astype(BF16))
            value = dot(hidden, e2[layer])
            message[rows, :] = (value * inverse_scale(value)).astype(BF16)

    outgoing[...] = dot(pick[...], sent).astype(BF16).reshape(n, cap, width)
    send(0)
    pick_sum[...] = dot(pick[...], recv_hot_t[...]).astype(BF16)
    picked[...] = dot(pick[...], nodes_ref[...]).astype(BF16)
    prepare(0)
    if layers > 1:
        prepare_picked(0)

    def run_layer(layer, carry):
        arrivals(layer)
        summed = picked_base[...] + dot(pick_sum[...], message[...])
        hidden = silu(picked_part[...] + dot(summed.astype(BF16), n1[layer, width:, :])).astype(BF16)
        update = dot(hidden, n2[layer])
        turned = dot(hidden, mixed[layer])
        scale = inverse_scale(update)
        sent = picked_sent[...] + (0.5 * scale) * turned
        outgoing[...] = sent.astype(BF16).reshape(n, cap, width)
        send(layer + 1)
        picked[...] = (picked[...].astype(F32) + scale * update).astype(BF16)
        for start in range(0, edge_rows, ROWS):
            rows = slice(start, start + ROWS)
            edges[rows, :] = (edges[rows, :].astype(F32) + message[rows, :].astype(F32)).astype(BF16)
        summed = dot(recv_hot_t[...], edges[...]).astype(BF16)
        nodes = nodes_ref[...]
        before = dot(nodes, n1[layer, :width, :]) + dot(summed, n1[layer, width:, :])
        update = dot(silu(before).astype(BF16), n2[layer])
        nodes_ref[...] = (nodes.astype(F32) + update * inverse_scale(update)).astype(BF16)
        prepare(layer + 1)
        prepare_picked(lax.min(layer + 1, layers - 2))
        return carry

    lax.fori_loop(0, layers - 1, run_layer, 0)

    last = layers - 1
    nodes = nodes_ref[...]
    base = dot(recv_hot_t[...], edges[...])
    part = dot(nodes, n1[last, :width, :])
    arrivals(last)
    summed = base + dot(recv_hot_t[...], message[...])
    hidden = silu(part + dot(summed.astype(BF16), n1[last, width:, :])).astype(BF16)
    update = dot(hidden, n2[last])
    out[...] = (nodes.astype(F32) + update * inverse_scale(update)).astype(BF16)

    several(table_send.at[pl.ds(0, n - 1)], table_send_sem).wait()

    @pl.when(me > 0)
    def _():
        part_copy(0, below).wait_send()

    @pl.when(me < n - 1)
    def _():
        part_copy(1, above).wait_send()


def shards(n, *args):
    grid_feats, mesh_embed, edge_latent = args[:3]
    grid_node, fetch_table, edge_sender, edge_receiver, block_count = args[3:8]
    weights = args[8:]
    grid_node = grid_node.reshape(-1, LANES)
    edge_sender = edge_sender.reshape(-1, LANES)
    edge_receiver = edge_receiver.reshape(-1, LANES)
    grid_feats = grid_feats.T
    grid_rows = grid_feats.shape[1]
    edge_rows = edge_latent.shape[0]
    nodes_dev, width = mesh_embed.shape
    cap = fetch_table.shape[2]
    layers = weights[3].shape[0]
    anywhere = pl.BlockSpec(memory_space=pltpu.HBM)

    def like(array):
        return pltpu.VMEM(array.shape, array.dtype)

    return pl.pallas_call(
        functools.partial(kernel, n),
        out_shape=pltpu.VMEM(mesh_embed.shape, mesh_embed.dtype),
        in_specs=[anywhere] * 15,
        out_specs=pl.BlockSpec(memory_space=pltpu.VMEM),
        scratch_shapes=[
            like(grid_feats),
            like(weights[0]),
            pltpu.VMEM(weights[0].shape[::-1], BF16),
            like(mesh_embed),
            *[like(weight) for weight in weights[1:]],
            like(edge_latent),
            like(grid_node),
            pltpu.VMEM(fetch_table.shape[1:], jnp.int32),
            like(edge_sender),
            like(edge_receiver),
            pltpu.SMEM(block_count.shape, block_count.dtype),
            pltpu.VMEM((3 * nodes_dev, grid_rows), BF16),
            pltpu.VMEM((width, grid_rows), BF16),
            pltpu.VMEM((2, nodes_dev, width), BF16),
            pltpu.VMEM((2, nodes_dev, width), BF16),
            pltpu.VMEM((n, 1, LANES), jnp.int32),
            pltpu.VMEM((n, 1, LANES), jnp.int32),
            pltpu.VMEM((n * cap, nodes_dev), BF16),
            pltpu.VMEM((n * cap, edge_rows), BF16),
            pltpu.VMEM((edge_rows, n * cap), BF16),
            pltpu.VMEM((edge_rows, nodes_dev), BF16),
            pltpu.VMEM((nodes_dev, edge_rows), BF16),
            pltpu.VMEM((edge_rows, width), F32),
            pltpu.VMEM((edge_rows, width), BF16),
            pltpu.VMEM((nodes_dev, width), BF16),
            pltpu.VMEM((n * cap, width), BF16),
            pltpu.VMEM((n * cap, width), F32),
            pltpu.VMEM((n * cap, width), F32),
            pltpu.VMEM((n * cap, width), F32),
            pltpu.VMEM((layers, width, width), BF16),
            pltpu.VMEM((n, cap, width), BF16),
            pltpu.VMEM((2, n, cap, width), BF16),
            pltpu.SemaphoreType.DMA((15,)),
            pltpu.SemaphoreType.DMA((2,)),
            pltpu.SemaphoreType.DMA((2,)),
            pltpu.SemaphoreType.DMA,
            pltpu.SemaphoreType.DMA,
            pltpu.SemaphoreType.DMA,
            pltpu.SemaphoreType.DMA((2,)),
        ],
        compiler_params=pltpu.CompilerParams(
            collective_id=0, has_side_effects=True, vmem_limit_bytes=66_900_000
        ),
        name="graph_net",
    )(
        grid_feats,
        mesh_embed,
        edge_latent,
        grid_node,
        fetch_table,
        edge_sender,
        edge_receiver,
        block_count,
        *weights,
    )


def solution(mesh):
    return jax.shard_map(
        functools.partial(shards, mesh.shape["band"]),
        mesh=mesh,
        in_specs=(
            P(("groups", "band"), None),
            P(("groups", "band"), None),
            P(("groups", "band"), None),
            P("band"),
            P("band", None, None),
            P("band"),
            P("band"),
            P("band"),
            P(),
            P(),
            P(),
            P(),
            P(),
            P(),
            P(),
        ),
        out_specs=P(("groups", "band"), None),
        check_vma=False,
    )
```

```python
import functools

import jax
import jax.numpy as jnp
from jax import lax
from jax.experimental import pallas as pl
from jax.experimental.pallas import tpu as pltpu
from jax.sharding import PartitionSpec as P

EDGE_BLOCK = 128
LANES = 128
ROWS = 256
CHUNK = 512
F32 = jnp.float32
BF16 = jnp.bfloat16


def silu_of_half(half):
    return half + half * jnp.tanh(half)


def silu(value):
    return silu_of_half(value * 0.5)


def center(weight):
    value = weight.astype(F32)
    return (value - jnp.mean(value, axis=-1, keepdims=True)).astype(BF16)


def inverse_scale(value):
    var = jnp.sum(value * value, axis=-1, keepdims=True) * (1.0 / value.shape[-1])
    return lax.rsqrt(var + 1e-05)


def dot(left, right):
    return jnp.dot(left, right, preferred_element_type=F32)


def peer_order(me, n):
    if n & (n - 1):
        return [lax.rem(me + step, n) for step in range(1, n)]
    peers = [0]
    place = 1
    while place < n:
        bit = lax.rem(lax.div(me, place), 2)
        same, other = bit * place, (1 - bit) * place
        peers = [low + same for low in peers] + [low + other for low in peers]
        place *= 2
    return peers[:0:-1]


def slot_of(owner, me, n):
    if n & (n - 1):
        return lax.rem(owner - me + 2 * n - 1, n)
    return (n - 1) - lax.bitwise_xor(owner, jnp.full(owner.shape, me, jnp.int32))


def kernel(
    n,
    grid_feats,
    mesh_embed,
    edge_latent,
    grid_node,
    fetch_table,
    edge_sender,
    edge_receiver,
    block_count,
    w_grid,
    enc_w1,
    enc_w2,
    edge_w1,
    edge_w2,
    node_w1,
    node_w2,
    out,
    gf,
    wg,
    wg_t,
    me_v,
    ew1,
    ew2,
    e1,
    e2,
    n1,
    n2,
    edges,
    gn,
    table,
    es,
    er,
    count,
    grid_hot,
    latent,
    part_send,
    part_recv,
    table_send,
    table_recv,
    pick,
    pick_sum,
    send_hot,
    recv_hot,
    recv_hot_t,
    local,
    message,
    turned_message,
    nodes_ref,
    picked,
    picked_part,
    picked_sent,
    mixed,
    joint,
    outgoing,
    incoming,
    load_sem,
    part_send_sem,
    part_recv_sem,
    table_send_sem,
    table_recv_sem,
    send_sem,
    recv_sem,
):
    me = lax.axis_index("band")
    nodes_dev, width = mesh_embed.shape
    layers = edge_w1.shape[0]
    cap = fetch_table.shape[2]
    edge_rows = edge_latent.shape[0]
    grid_rows = grid_feats.shape[1]

    peers = peer_order(me, n)
    barrier = pltpu.get_barrier_semaphore()
    for peer in peers:
        pl.semaphore_signal(barrier, inc=1, device_id={"band": peer})

    pairs = [
        (grid_node, gn),
        (w_grid, wg),
        (grid_feats, gf),
        (fetch_table.at[0], table),
        (edge_sender, es),
        (edge_receiver, er),
        (block_count, count),
        (mesh_embed, me_v),
        (enc_w1, ew1),
        (enc_w2, ew2),
        (edge_w1, e1),
        (edge_latent, edges),
        (node_w2, n2),
        (edge_w2, e2),
        (node_w1, n1),
    ]
    loads = [
        pltpu.make_async_copy(source, target, load_sem.at[index])
        for index, (source, target) in enumerate(pairs)
    ]
    for load in loads[:7]:
        load.start()

    loads[0].wait()
    first = (me - 1) * nodes_dev
    for row in range(grid_rows // LANES):
        column = gn[row : row + 1, :] - first
        hot = lax.broadcasted_iota(jnp.int32, (3 * nodes_dev, LANES), 0) == column
        grid_hot[:, row * LANES : (row + 1) * LANES] = hot.astype(F32).astype(BF16)
    loads[3].wait()
    for owner in range(n):
        table_send[owner, :, :cap] = table[owner : owner + 1, :]
    table_recv[n - 1] = table_send[me]
    loads[1].wait()
    wg_t[...] = wg[...].T
    loads[2].wait()
    for load in loads[7:]:
        load.start()
    for start in range(0, grid_rows, ROWS):
        rows = slice(start, start + ROWS)
        latent[:, rows] = silu(dot(wg_t[...], gf[:, rows])).astype(BF16)
    partial = lax.dot_general(
        grid_hot[...], latent[...], (((1,), (1,)), ((), ())), preferred_element_type=F32
    )
    part_send[0] = partial[:nodes_dev].astype(BF16)
    part_send[1] = partial[2 * nodes_dev :].astype(BF16)
    own = partial[nodes_dev : 2 * nodes_dev]

    pl.semaphore_wait(barrier, n - 1)

    def part_copy(slot, target):
        return pltpu.make_async_remote_copy(
            src_ref=part_send.at[slot],
            dst_ref=part_recv.at[slot],
            send_sem=part_send_sem.at[slot],
            recv_sem=part_recv_sem.at[slot],
            device_id={"band": target},
        )

    below = lax.rem(me + n - 1, n)
    above = lax.rem(me + 1, n)
    down = part_copy(0, below)
    up = part_copy(1, above)

    def table_copy(slot, peer):
        return pltpu.make_async_remote_copy(
            src_ref=table_send.at[peer],
            dst_ref=table_recv.at[slot],
            send_sem=table_send_sem,
            recv_sem=table_recv_sem,
            device_id={"band": peer},
        )

    half = n // 2
    for slot in range(half):
        table_copy(slot, peers[slot]).start()

    @pl.when(me > 0)
    def _():
        down.start()

    @pl.when(me < n - 1)
    def _():
        up.start()

    for slot in range(half, n - 1):
        table_copy(slot, peers[slot]).start()

    loads[4].wait()
    loads[5].wait()
    loads[6].wait()
    live_rows = count[0] * EDGE_BLOCK
    slots = es[...]
    owner = lax.div(slots, cap)
    slots = slot_of(owner, me, n) * cap + (slots - owner * cap)
    for row in range(edge_rows // LANES):
        rows = slice(row * LANES, (row + 1) * LANES)
        lane = lax.broadcasted_iota(jnp.int32, (LANES, LANES), 1)
        sender = jnp.broadcast_to(slots[row : row + 1, :], (LANES, LANES)).T
        for base in range(0, n * cap, LANES):
            hot = (sender == lane + base).astype(F32).astype(BF16)
            send_hot[rows, base : base + LANES] = hot
        value = er[row : row + 1, :]
        receiver = jnp.broadcast_to(value, (LANES, LANES)).T
        for base in range(0, nodes_dev, LANES):
            hot = (receiver == lane + base).astype(F32).astype(BF16)
            recv_hot[rows, base : base + LANES] = hot
        place = lax.broadcasted_iota(jnp.int32, (1, LANES), 1) + row * LANES
        masked = jnp.where(place < live_rows, value, -1)
        hot = lax.broadcasted_iota(jnp.int32, (nodes_dev, LANES), 0) == masked
        recv_hot_t[:, rows] = hot.astype(F32).astype(BF16)

    def sender_weight(layer):
        return e1[layer, width : 2 * width, :]

    for index in range(7, 15):
        loads[index].wait()
    ew2[...] = center(ew2[...])
    mixed[layers - 1] = dot(ew2[...], sender_weight(0)).astype(BF16)
    embed_sent = dot(me_v[...], sender_weight(0)) * 0.5
    for layer in range(layers):
        e2[layer] = center(e2[layer])
        n2[layer] = center(n2[layer])
        joint[layer] = dot(e2[layer], n1[layer, width:, :]).astype(BF16)
    for layer in range(layers - 1):
        mixed[layer] = dot(n2[layer], sender_weight(layer + 1)).astype(BF16)

    @pl.when(me > 0)
    def _():
        part_copy(1, above).wait_recv()

    @pl.when(me == 0)
    def _():
        part_recv[1] = jnp.zeros((nodes_dev, width), BF16)

    @pl.when(me < n - 1)
    def _():
        part_copy(0, below).wait_recv()

    @pl.when(me == n - 1)
    def _():
        part_recv[0] = jnp.zeros((nodes_dev, width), BF16)

    agg = own + part_recv[0].astype(F32) + part_recv[1].astype(F32)
    hidden = silu(dot(agg.astype(BF16), ew1[...])).astype(BF16)
    update = dot(hidden, ew2[...])
    turned = dot(hidden, mixed[layers - 1])
    scale = inverse_scale(update)
    sent = (embed_sent + (0.5 * scale) * turned).astype(BF16)
    nodes_ref[...] = (me_v[...].astype(F32) + scale * update).astype(BF16)

    def several(refs, sems):
        return pltpu.make_async_copy(refs, refs, sems)

    several(table_recv.at[pl.ds(0, n - 1)], table_recv_sem).wait()
    def choose(first, size):
        rows = slice(first * cap, (first + size) * cap)
        wanted = jnp.broadcast_to(table_recv[first : first + size], (size, cap, LANES))
        wanted = wanted.reshape(size * cap, LANES)
        slot = lax.rem(lax.broadcasted_iota(jnp.int32, (size * cap, LANES), 0), cap)
        lane = lax.broadcasted_iota(jnp.int32, (size * cap, LANES), 1)
        column = jnp.sum(jnp.where(slot == lane, wanted, 0).astype(F32), axis=1, keepdims=True)
        lane = lax.broadcasted_iota(jnp.int32, (size * cap, nodes_dev), 1).astype(F32)
        pick[rows, :] = (column == lane).astype(F32).astype(BF16)
        chosen = dot(pick[rows, :], sent).astype(BF16)
        outgoing[first : first + size] = chosen.reshape(size, cap, width)

    def layer_copy(layer, slot, peer):
        return pltpu.make_async_remote_copy(
            src_ref=outgoing.at[slot],
            dst_ref=incoming.at[lax.rem(layer, 2), slot],
            send_sem=send_sem,
            recv_sem=recv_sem.at[lax.rem(layer, 2)],
            device_id={"band": peer},
        )

    def send(layer, slots):
        for slot in slots:
            layer_copy(layer, slot, peers[slot]).start()

    def keep(layer):
        incoming[lax.rem(layer, 2), n - 1] = outgoing[n - 1]

    def prepare(layer):
        nodes = nodes_ref[...]
        kept = dot(nodes, e1[layer, 2 * width :, :]).astype(BF16)
        for start in range(0, edge_rows, ROWS):
            rows = slice(start, start + ROWS)
            joined = dot(edges[rows, :], e1[layer, :width, :]) + dot(recv_hot[rows, :], kept)
            local[rows, :] = joined * 0.5

    def prepare_picked(layer):
        base = dot(pick_sum[...], edges[...]).astype(BF16)
        part = dot(picked[...], n1[layer, :width, :])
        picked_part[...] = part + dot(base, n1[layer, width:, :])
        picked_sent[...] = dot(picked[...], sender_weight(layer + 1)) * 0.5

    def arrivals(layer):
        parity = lax.rem(layer, 2)
        several(incoming.at[parity, pl.ds(0, n - 1)], recv_sem.at[parity]).wait()
        several(outgoing.at[pl.ds(0, n - 1)], send_sem).wait()
        senders = incoming[parity].reshape(n * cap, width)
        pieces = [slice(start, start + CHUNK) for start in range(0, edge_rows, CHUNK)]
        hiddens = {}
        values = {}
        turned = {}
        for step in range(len(pieces) + 2):
            if step < len(pieces):
                rows = pieces[step]
                before = local[rows, :] + dot(send_hot[rows, :], senders)
                hiddens[step] = silu_of_half(before.astype(BF16))
            if 0 <= step - 1 < len(pieces):
                values[step - 1] = dot(hiddens[step - 1], e2[layer])
                turned[step - 1] = dot(hiddens[step - 1], joint[layer])
            if 0 <= step - 2:
                rows = pieces[step - 2]
                value = values[step - 2]
                message[rows, :] = value.astype(BF16)
                turned_message[rows, :] = (turned[step - 2] * inverse_scale(value)).astype(BF16)

    groups = ((0, half), (half, n - half))
    for first, size in groups:
        choose(first, size)
        send(0, range(first, min(first + size, n - 1)))
    keep(0)
    pick_sum[...] = dot(pick[...], recv_hot_t[...]).astype(BF16)
    picked[...] = dot(pick[...], nodes_ref[...]).astype(BF16)
    prepare(0)
    if layers > 1:
        prepare_picked(0)

    def run_layer(layer, carry):
        arrivals(layer)
        for first, size in groups:
            rows = slice(first * cap, (first + size) * cap)
            before = picked_part[rows, :] + dot(pick_sum[rows, :], turned_message[...])
            hidden = silu(before).astype(BF16)
            update = dot(hidden, n2[layer])
            turned = dot(hidden, mixed[layer])
            scale = inverse_scale(update)
            sent = picked_sent[rows, :] + (0.5 * scale) * turned
            outgoing[first : first + size] = sent.astype(BF16).reshape(size, cap, width)
            send(layer + 1, range(first, min(first + size, n - 1)))
            picked[rows, :] = (picked[rows, :].astype(F32) + scale * update).astype(BF16)
        keep(layer + 1)
        for start in range(0, edge_rows, ROWS):
            rows = slice(start, start + ROWS)
            value = message[rows, :].astype(F32)
            value = value * inverse_scale(value)
            edges[rows, :] = (edges[rows, :].astype(F32) + value).astype(BF16)
        summed = dot(recv_hot_t[...], edges[...]).astype(BF16)
        nodes = nodes_ref[...]
        before = dot(nodes, n1[layer, :width, :]) + dot(summed, n1[layer, width:, :])
        update = dot(silu(before).astype(BF16), n2[layer])
        nodes_ref[...] = (nodes.astype(F32) + update * inverse_scale(update)).astype(BF16)
        prepare(layer + 1)
        prepare_picked(lax.min(layer + 1, layers - 2))
        return carry

    lax.fori_loop(0, layers - 1, run_layer, 0)

    last = layers - 1
    nodes = nodes_ref[...]
    base = dot(recv_hot_t[...], edges[...]).astype(BF16)
    part = dot(nodes, n1[last, :width, :]) + dot(base, n1[last, width:, :])
    arrivals(last)
    hidden = silu(part + dot(recv_hot_t[...], turned_message[...])).astype(BF16)
    update = dot(hidden, n2[last])
    out[...] = (nodes.astype(F32) + update * inverse_scale(update)).astype(BF16)

    several(table_send.at[pl.ds(0, n - 1)], table_send_sem).wait()

    @pl.when(me > 0)
    def _():
        part_copy(0, below).wait_send()

    @pl.when(me < n - 1)
    def _():
        part_copy(1, above).wait_send()


def shards(n, *args):
    grid_feats, mesh_embed, edge_latent = args[:3]
    grid_node, fetch_table, edge_sender, edge_receiver, block_count = args[3:8]
    weights = args[8:]
    grid_node = grid_node.reshape(-1, LANES)
    edge_sender = edge_sender.reshape(-1, LANES)
    edge_receiver = edge_receiver.reshape(-1, LANES)
    grid_feats = grid_feats.T
    grid_rows = grid_feats.shape[1]
    edge_rows = edge_latent.shape[0]
    nodes_dev, width = mesh_embed.shape
    cap = fetch_table.shape[2]
    layers = weights[3].shape[0]
    anywhere = pl.BlockSpec(memory_space=pltpu.HBM)

    def like(array):
        return pltpu.VMEM(array.shape, array.dtype)

    return pl.pallas_call(
        functools.partial(kernel, n),
        out_shape=pltpu.VMEM(mesh_embed.shape, mesh_embed.dtype),
        in_specs=[anywhere] * 15,
        out_specs=pl.BlockSpec(memory_space=pltpu.VMEM),
        scratch_shapes=[
            like(grid_feats),
            like(weights[0]),
            pltpu.VMEM(weights[0].shape[::-1], BF16),
            like(mesh_embed),
            *[like(weight) for weight in weights[1:]],
            like(edge_latent),
            like(grid_node),
            pltpu.VMEM(fetch_table.shape[1:], jnp.int32),
            like(edge_sender),
            like(edge_receiver),
            pltpu.SMEM(block_count.shape, block_count.dtype),
            pltpu.VMEM((3 * nodes_dev, grid_rows), BF16),
            pltpu.VMEM((width, grid_rows), BF16),
            pltpu.VMEM((2, nodes_dev, width), BF16),
            pltpu.VMEM((2, nodes_dev, width), BF16),
            pltpu.VMEM((n, 1, LANES), jnp.int32),
            pltpu.VMEM((n, 1, LANES), jnp.int32),
            pltpu.VMEM((n * cap, nodes_dev), BF16),
            pltpu.VMEM((n * cap, edge_rows), BF16),
            pltpu.VMEM((edge_rows, n * cap), BF16),
            pltpu.VMEM((edge_rows, nodes_dev), BF16),
            pltpu.VMEM((nodes_dev, edge_rows), BF16),
            pltpu.VMEM((edge_rows, width), F32),
            pltpu.VMEM((edge_rows, width), BF16),
            pltpu.VMEM((edge_rows, width), BF16),
            pltpu.VMEM((nodes_dev, width), BF16),
            pltpu.VMEM((n * cap, width), BF16),
            pltpu.VMEM((n * cap, width), F32),
            pltpu.VMEM((n * cap, width), F32),
            pltpu.VMEM((layers, width, width), BF16),
            pltpu.VMEM((layers, width, width), BF16),
            pltpu.VMEM((n, cap, width), BF16),
            pltpu.VMEM((2, n, cap, width), BF16),
            pltpu.SemaphoreType.DMA((15,)),
            pltpu.SemaphoreType.DMA((2,)),
            pltpu.SemaphoreType.DMA((2,)),
            pltpu.SemaphoreType.DMA,
            pltpu.SemaphoreType.DMA,
            pltpu.SemaphoreType.DMA,
            pltpu.SemaphoreType.DMA((2,)),
        ],
        compiler_params=pltpu.CompilerParams(
            collective_id=0, has_side_effects=True, vmem_limit_bytes=66_900_000
        ),
        name="graph_net",
    )(
        grid_feats,
        mesh_embed,
        edge_latent,
        grid_node,
        fetch_table,
        edge_sender,
        edge_receiver,
        block_count,
        *weights,
    )


def solution(mesh):
    return jax.shard_map(
        functools.partial(shards, mesh.shape["band"]),
        mesh=mesh,
        in_specs=(
            P(("groups", "band"), None),
            P(("groups", "band"), None),
            P(("groups", "band"), None),
            P("band"),
            P("band", None, None),
            P("band"),
            P("band"),
            P("band"),
            P(),
            P(),
            P(),
            P(),
            P(),
            P(),
            P(),
        ),
        out_specs=P(("groups", "band"), None),
        check_vma=False,
    )
```

```python
import functools

import jax
import jax.numpy as jnp
from jax import lax
from jax.experimental import pallas as pl
from jax.experimental.pallas import tpu as pltpu
from jax.sharding import PartitionSpec as P

EDGE_BLOCK = 128
LANES = 128
ROWS = 256
CHUNK = 512
F32 = jnp.float32
BF16 = jnp.bfloat16


def silu_of_half(half):
    return half + half * jnp.tanh(half)


def silu(value):
    return silu_of_half(value * 0.5)


def center(weight):
    value = weight.astype(F32)
    return (value - jnp.mean(value, axis=-1, keepdims=True)).astype(BF16)


def inverse_scale(value):
    var = jnp.sum(value * value, axis=-1, keepdims=True) * (1.0 / value.shape[-1])
    return lax.rsqrt(var + 1e-05)


def dot(left, right):
    return jnp.dot(left, right, preferred_element_type=F32)


def flipped(me, bits):
    place, result = 1, 0
    while place <= bits or place == 1:
        bit = lax.rem(lax.div(me, place), 2)
        result += place * ((1 - bit if bits & place else bit) - bit)
        place *= 2
    return me + result


def peer_order(me, n):
    assert n & (n - 1) == 0
    return [flipped(me, bits) for bits in sorted(range(1, n), key=lambda bits: (-(bits >= n // 2), bits & 1, -bits))]


def slot_of(owner, peers):
    slot = jnp.full(owner.shape, len(peers), jnp.int32)
    for place, peer in enumerate(peers):
        slot = jnp.where(owner == peer, place, slot)
    return slot


def kernel(
    n,
    grid_feats,
    mesh_embed,
    edge_latent,
    grid_node,
    fetch_table,
    edge_sender,
    edge_receiver,
    block_count,
    w_grid,
    enc_w1,
    enc_w2,
    edge_w1,
    edge_w2,
    node_w1,
    node_w2,
    out,
    gf,
    wg,
    wg_t,
    me_v,
    ew1,
    ew2,
    e1,
    e2,
    n1,
    n2,
    edges,
    gn,
    table,
    es,
    er,
    count,
    grid_hot,
    latent,
    part_send,
    part_recv,
    table_send,
    table_recv,
    pick,
    pick_sum,
    send_hot,
    recv_hot,
    recv_hot_t,
    local,
    message,
    turned_message,
    nodes_ref,
    picked,
    picked_part,
    picked_sent,
    mixed,
    joint,
    outgoing,
    incoming,
    load_sem,
    part_send_sem,
    part_recv_sem,
    table_send_sem,
    table_recv_sem,
    send_sem,
    recv_sem,
):
    me = lax.axis_index("band")
    nodes_dev, width = mesh_embed.shape
    layers = edge_w1.shape[0]
    cap = fetch_table.shape[2]
    edge_rows = edge_latent.shape[0]
    grid_rows = grid_feats.shape[1]

    peers = peer_order(me, n)
    barrier = pltpu.get_barrier_semaphore()
    for peer in peers:
        pl.semaphore_signal(barrier, inc=1, device_id={"band": peer})

    pairs = [
        (grid_node, gn),
        (w_grid, wg),
        (grid_feats, gf),
        (fetch_table.at[0], table),
        (edge_sender, es),
        (edge_receiver, er),
        (block_count, count),
        (mesh_embed, me_v),
        (enc_w1, ew1),
        (enc_w2, ew2),
        (edge_w1, e1),
        (edge_latent, edges),
        (node_w2, n2),
        (edge_w2, e2),
        (node_w1, n1),
    ]
    loads = [
        pltpu.make_async_copy(source, target, load_sem.at[index])
        for index, (source, target) in enumerate(pairs)
    ]
    for load in loads[:7]:
        load.start()

    loads[0].wait()
    first = (me - 1) * nodes_dev
    for row in range(grid_rows // LANES):
        column = gn[row : row + 1, :] - first
        hot = lax.broadcasted_iota(jnp.int32, (3 * nodes_dev, LANES), 0) == column
        grid_hot[:, row * LANES : (row + 1) * LANES] = hot.astype(F32).astype(BF16)
    loads[3].wait()
    for owner in range(n):
        table_send[owner, :, :cap] = table[owner : owner + 1, :]
    table_recv[n - 1] = table_send[me]
    loads[1].wait()
    wg_t[...] = wg[...].T
    loads[2].wait()
    for load in loads[7:]:
        load.start()
    for start in range(0, grid_rows, ROWS):
        rows = slice(start, start + ROWS)
        latent[:, rows] = silu(dot(wg_t[...], gf[:, rows])).astype(BF16)
    partial = lax.dot_general(
        grid_hot[...], latent[...], (((1,), (1,)), ((), ())), preferred_element_type=F32
    )
    part_send[0] = partial[:nodes_dev].astype(BF16)
    part_send[1] = partial[2 * nodes_dev :].astype(BF16)
    own = partial[nodes_dev : 2 * nodes_dev]

    pl.semaphore_wait(barrier, n - 1)

    def part_copy(slot, target):
        return pltpu.make_async_remote_copy(
            src_ref=part_send.at[slot],
            dst_ref=part_recv.at[slot],
            send_sem=part_send_sem.at[slot],
            recv_sem=part_recv_sem.at[slot],
            device_id={"band": target},
        )

    below = lax.rem(me + n - 1, n)
    above = lax.rem(me + 1, n)
    down = part_copy(0, below)
    up = part_copy(1, above)

    def table_copy(slot, peer):
        return pltpu.make_async_remote_copy(
            src_ref=table_send.at[peer],
            dst_ref=table_recv.at[slot],
            send_sem=table_send_sem,
            recv_sem=table_recv_sem,
            device_id={"band": peer},
        )

    half = n // 2
    for slot in range(half):
        table_copy(slot, peers[slot]).start()

    @pl.when(me > 0)
    def _():
        down.start()

    @pl.when(me < n - 1)
    def _():
        up.start()

    for slot in range(half, n - 1):
        table_copy(slot, peers[slot]).start()

    loads[4].wait()
    loads[5].wait()
    loads[6].wait()
    live_rows = count[0] * EDGE_BLOCK
    slots = es[...]
    owner = lax.div(slots, cap)
    slots = slot_of(owner, peers) * cap + (slots - owner * cap)
    for row in range(edge_rows // LANES):
        rows = slice(row * LANES, (row + 1) * LANES)
        lane = lax.broadcasted_iota(jnp.int32, (LANES, LANES), 1)
        sender = jnp.broadcast_to(slots[row : row + 1, :], (LANES, LANES)).T
        for base in range(0, n * cap, LANES):
            hot = (sender == lane + base).astype(F32).astype(BF16)
            send_hot[rows, base : base + LANES] = hot
        value = er[row : row + 1, :]
        receiver = jnp.broadcast_to(value, (LANES, LANES)).T
        for base in range(0, nodes_dev, LANES):
            hot = (receiver == lane + base).astype(F32).astype(BF16)
            recv_hot[rows, base : base + LANES] = hot
        place = lax.broadcasted_iota(jnp.int32, (1, LANES), 1) + row * LANES
        masked = jnp.where(place < live_rows, value, -1)
        hot = lax.broadcasted_iota(jnp.int32, (nodes_dev, LANES), 0) == masked
        recv_hot_t[:, rows] = hot.astype(F32).astype(BF16)

    def sender_weight(layer):
        return e1[layer, width : 2 * width, :]

    for index in range(7, 15):
        loads[index].wait()
    ew2[...] = center(ew2[...])
    mixed[layers - 1] = dot(ew2[...], sender_weight(0)).astype(BF16)
    embed_sent = dot(me_v[...], sender_weight(0)) * 0.5
    for layer in range(layers):
        e2[layer] = center(e2[layer])
        n2[layer] = center(n2[layer])
        joint[layer] = dot(e2[layer], n1[layer, width:, :]).astype(BF16)
    for layer in range(layers - 1):
        mixed[layer] = dot(n2[layer], sender_weight(layer + 1)).astype(BF16)

    @pl.when(me > 0)
    def _():
        part_copy(1, above).wait_recv()

    @pl.when(me == 0)
    def _():
        part_recv[1] = jnp.zeros((nodes_dev, width), BF16)

    @pl.when(me < n - 1)
    def _():
        part_copy(0, below).wait_recv()

    @pl.when(me == n - 1)
    def _():
        part_recv[0] = jnp.zeros((nodes_dev, width), BF16)

    agg = own + part_recv[0].astype(F32) + part_recv[1].astype(F32)
    hidden = silu(dot(agg.astype(BF16), ew1[...])).astype(BF16)
    update = dot(hidden, ew2[...])
    turned = dot(hidden, mixed[layers - 1])
    scale = inverse_scale(update)
    sent = (embed_sent + (0.5 * scale) * turned).astype(BF16)
    nodes_ref[...] = (me_v[...].astype(F32) + scale * update).astype(BF16)

    def several(refs, sems):
        return pltpu.make_async_copy(refs, refs, sems)

    several(table_recv.at[pl.ds(0, n - 1)], table_recv_sem).wait()
    def choose(first, size):
        rows = slice(first * cap, (first + size) * cap)
        wanted = jnp.broadcast_to(table_recv[first : first + size], (size, cap, LANES))
        wanted = wanted.reshape(size * cap, LANES)
        slot = lax.rem(lax.broadcasted_iota(jnp.int32, (size * cap, LANES), 0), cap)
        lane = lax.broadcasted_iota(jnp.int32, (size * cap, LANES), 1)
        column = jnp.sum(jnp.where(slot == lane, wanted, 0).astype(F32), axis=1, keepdims=True)
        lane = lax.broadcasted_iota(jnp.int32, (size * cap, nodes_dev), 1).astype(F32)
        pick[rows, :] = (column == lane).astype(F32).astype(BF16)
        chosen = dot(pick[rows, :], sent).astype(BF16)
        outgoing[first : first + size] = chosen.reshape(size, cap, width)

    def layer_copy(layer, slot, peer):
        return pltpu.make_async_remote_copy(
            src_ref=outgoing.at[slot],
            dst_ref=incoming.at[lax.rem(layer, 2), slot],
            send_sem=send_sem,
            recv_sem=recv_sem.at[lax.rem(layer, 2)],
            device_id={"band": peer},
        )

    def send(layer, slots):
        for slot in slots:
            layer_copy(layer, slot, peers[slot]).start()

    def keep(layer):
        incoming[lax.rem(layer, 2), n - 1] = outgoing[n - 1]

    def prepare(layer):
        nodes = nodes_ref[...]
        kept = dot(nodes, e1[layer, 2 * width :, :]).astype(BF16)
        for start in range(0, edge_rows, ROWS):
            rows = slice(start, start + ROWS)
            joined = dot(edges[rows, :], e1[layer, :width, :]) + dot(recv_hot[rows, :], kept)
            local[rows, :] = joined * 0.5

    def prepare_picked(layer):
        base = dot(pick_sum[...], edges[...]).astype(BF16)
        part = dot(picked[...], n1[layer, :width, :])
        picked_part[...] = part + dot(base, n1[layer, width:, :])
        picked_sent[...] = dot(picked[...], sender_weight(layer + 1)) * 0.5

    def arrivals(layer):
        parity = lax.rem(layer, 2)
        several(incoming.at[parity, pl.ds(0, n - 1)], recv_sem.at[parity]).wait()
        several(outgoing.at[pl.ds(0, n - 1)], send_sem).wait()
        senders = incoming[parity].reshape(n * cap, width)
        pieces = [slice(start, start + CHUNK) for start in range(0, edge_rows, CHUNK)]
        hiddens = {}
        values = {}
        turned = {}
        for step in range(len(pieces) + 2):
            if step < len(pieces):
                rows = pieces[step]
                before = local[rows, :] + dot(send_hot[rows, :], senders)
                hiddens[step] = silu_of_half(before.astype(BF16))
            if 0 <= step - 1 < len(pieces):
                values[step - 1] = dot(hiddens[step - 1], e2[layer])
                turned[step - 1] = dot(hiddens[step - 1], joint[layer])
            if 0 <= step - 2:
                rows = pieces[step - 2]
                value = values[step - 2]
                message[rows, :] = value.astype(BF16)
                turned_message[rows, :] = (turned[step - 2] * inverse_scale(value)).astype(BF16)

    groups = ((0, half), (half, n - half))
    for first, size in groups:
        choose(first, size)
        send(0, range(first, min(first + size, n - 1)))
    keep(0)
    pick_sum[...] = dot(pick[...], recv_hot_t[...]).astype(BF16)
    picked[...] = dot(pick[...], nodes_ref[...]).astype(BF16)
    prepare(0)
    if layers > 1:
        prepare_picked(0)

    def run_layer(layer, carry):
        arrivals(layer)
        for first, size in groups:
            rows = slice(first * cap, (first + size) * cap)
            before = picked_part[rows, :] + dot(pick_sum[rows, :], turned_message[...])
            hidden = silu(before).astype(BF16)
            update = dot(hidden, n2[layer])
            turned = dot(hidden, mixed[layer])
            scale = inverse_scale(update)
            sent = picked_sent[rows, :] + (0.5 * scale) * turned
            outgoing[first : first + size] = sent.astype(BF16).reshape(size, cap, width)
            send(layer + 1, range(first, min(first + size, n - 1)))
            picked[rows, :] = (picked[rows, :].astype(F32) + scale * update).astype(BF16)
        keep(layer + 1)
        for start in range(0, edge_rows, ROWS):
            rows = slice(start, start + ROWS)
            value = message[rows, :].astype(F32)
            value = value * inverse_scale(value)
            edges[rows, :] = (edges[rows, :].astype(F32) + value).astype(BF16)
        summed = dot(recv_hot_t[...], edges[...]).astype(BF16)
        nodes = nodes_ref[...]
        before = dot(nodes, n1[layer, :width, :]) + dot(summed, n1[layer, width:, :])
        update = dot(silu(before).astype(BF16), n2[layer])
        nodes_ref[...] = (nodes.astype(F32) + update * inverse_scale(update)).astype(BF16)
        prepare(layer + 1)
        prepare_picked(lax.min(layer + 1, layers - 2))
        return carry

    lax.fori_loop(0, layers - 1, run_layer, 0)

    last = layers - 1
    nodes = nodes_ref[...]
    base = dot(recv_hot_t[...], edges[...]).astype(BF16)
    part = dot(nodes, n1[last, :width, :]) + dot(base, n1[last, width:, :])
    arrivals(last)
    hidden = silu(part + dot(recv_hot_t[...], turned_message[...])).astype(BF16)
    update = dot(hidden, n2[last])
    out[...] = (nodes.astype(F32) + update * inverse_scale(update)).astype(BF16)

    several(table_send.at[pl.ds(0, n - 1)], table_send_sem).wait()

    @pl.when(me > 0)
    def _():
        part_copy(0, below).wait_send()

    @pl.when(me < n - 1)
    def _():
        part_copy(1, above).wait_send()


def shards(n, *args):
    grid_feats, mesh_embed, edge_latent = args[:3]
    grid_node, fetch_table, edge_sender, edge_receiver, block_count = args[3:8]
    weights = args[8:]
    grid_node = grid_node.reshape(-1, LANES)
    edge_sender = edge_sender.reshape(-1, LANES)
    edge_receiver = edge_receiver.reshape(-1, LANES)
    grid_feats = grid_feats.T
    grid_rows = grid_feats.shape[1]
    edge_rows = edge_latent.shape[0]
    nodes_dev, width = mesh_embed.shape
    cap = fetch_table.shape[2]
    layers = weights[3].shape[0]
    anywhere = pl.BlockSpec(memory_space=pltpu.HBM)

    def like(array):
        return pltpu.VMEM(array.shape, array.dtype)

    return pl.pallas_call(
        functools.partial(kernel, n),
        out_shape=pltpu.VMEM(mesh_embed.shape, mesh_embed.dtype),
        in_specs=[anywhere] * 15,
        out_specs=pl.BlockSpec(memory_space=pltpu.VMEM),
        scratch_shapes=[
            like(grid_feats),
            like(weights[0]),
            pltpu.VMEM(weights[0].shape[::-1], BF16),
            like(mesh_embed),
            *[like(weight) for weight in weights[1:]],
            like(edge_latent),
            like(grid_node),
            pltpu.VMEM(fetch_table.shape[1:], jnp.int32),
            like(edge_sender),
            like(edge_receiver),
            pltpu.SMEM(block_count.shape, block_count.dtype),
            pltpu.VMEM((3 * nodes_dev, grid_rows), BF16),
            pltpu.VMEM((width, grid_rows), BF16),
            pltpu.VMEM((2, nodes_dev, width), BF16),
            pltpu.VMEM((2, nodes_dev, width), BF16),
            pltpu.VMEM((n, 1, LANES), jnp.int32),
            pltpu.VMEM((n, 1, LANES), jnp.int32),
            pltpu.VMEM((n * cap, nodes_dev), BF16),
            pltpu.VMEM((n * cap, edge_rows), BF16),
            pltpu.VMEM((edge_rows, n * cap), BF16),
            pltpu.VMEM((edge_rows, nodes_dev), BF16),
            pltpu.VMEM((nodes_dev, edge_rows), BF16),
            pltpu.VMEM((edge_rows, width), F32),
            pltpu.VMEM((edge_rows, width), BF16),
            pltpu.VMEM((edge_rows, width), BF16),
            pltpu.VMEM((nodes_dev, width), BF16),
            pltpu.VMEM((n * cap, width), BF16),
            pltpu.VMEM((n * cap, width), F32),
            pltpu.VMEM((n * cap, width), F32),
            pltpu.VMEM((layers, width, width), BF16),
            pltpu.VMEM((layers, width, width), BF16),
            pltpu.VMEM((n, cap, width), BF16),
            pltpu.VMEM((2, n, cap, width), BF16),
            pltpu.SemaphoreType.DMA((15,)),
            pltpu.SemaphoreType.DMA((2,)),
            pltpu.SemaphoreType.DMA((2,)),
            pltpu.SemaphoreType.DMA,
            pltpu.SemaphoreType.DMA,
            pltpu.SemaphoreType.DMA,
            pltpu.SemaphoreType.DMA((2,)),
        ],
        compiler_params=pltpu.CompilerParams(
            collective_id=0, has_side_effects=True, vmem_limit_bytes=66_900_000
        ),
        name="graph_net",
    )(
        grid_feats,
        mesh_embed,
        edge_latent,
        grid_node,
        fetch_table,
        edge_sender,
        edge_receiver,
        block_count,
        *weights,
    )


def solution(mesh):
    return jax.shard_map(
        functools.partial(shards, mesh.shape["band"]),
        mesh=mesh,
        in_specs=(
            P(("groups", "band"), None),
            P(("groups", "band"), None),
            P(("groups", "band"), None),
            P("band"),
            P("band", None, None),
            P("band"),
            P("band"),
            P("band"),
            P(),
            P(),
            P(),
            P(),
            P(),
            P(),
            P(),
        ),
        out_specs=P(("groups", "band"), None),
        check_vma=False,
    )
```

```python
import functools

import jax
import jax.numpy as jnp
from jax import lax
from jax.experimental import pallas as pl
from jax.experimental.pallas import tpu as pltpu
from jax.sharding import PartitionSpec as P

EDGE_BLOCK = 128
LANES = 128
ROWS = 256
CHUNK = 512
F32 = jnp.float32
BF16 = jnp.bfloat16


def silu_of_half(half):
    return half + half * jnp.tanh(half)


def silu(value):
    return silu_of_half(value * 0.5)


def center(weight):
    value = weight.astype(F32)
    return (value - jnp.mean(value, axis=-1, keepdims=True)).astype(BF16)


def inverse_scale(value):
    var = jnp.sum(value * value, axis=-1, keepdims=True) * (1.0 / value.shape[-1])
    return lax.rsqrt(var + 1e-05)


def dot(left, right):
    return jnp.dot(left, right, preferred_element_type=F32)


def flipped(me, bits):
    place, result = 1, 0
    while place <= bits or place == 1:
        bit = lax.rem(lax.div(me, place), 2)
        result += place * ((1 - bit if bits & place else bit) - bit)
        place *= 2
    return me + result


def peer_order(me, n):
    assert n & (n - 1) == 0
    return [flipped(me, bits) for bits in sorted(range(1, n), key=lambda bits: (-(bits >= n // 2), bits & 1, -bits))]


def slot_of(owner, peers):
    slot = jnp.full(owner.shape, len(peers), jnp.int32)
    for place, peer in enumerate(peers):
        slot = jnp.where(owner == peer, place, slot)
    return slot


def kernel(
    n,
    grid_feats,
    mesh_embed,
    edge_latent,
    grid_node,
    fetch_table,
    edge_sender,
    edge_receiver,
    block_count,
    w_grid,
    enc_w1,
    enc_w2,
    edge_w1,
    edge_w2,
    node_w1,
    node_w2,
    out,
    gf,
    wg,
    wg_t,
    me_v,
    ew1,
    ew2,
    e1,
    e2,
    n1,
    n2,
    edges,
    gn,
    table,
    es,
    er,
    count,
    grid_hot,
    latent,
    part_send,
    part_recv,
    table_send,
    table_recv,
    pick,
    pick_sum,
    send_hot,
    recv_hot,
    recv_hot_t,
    local,
    message,
    turned_message,
    nodes_ref,
    picked,
    picked_part,
    picked_sent,
    mixed,
    joint,
    outgoing,
    incoming,
    load_sem,
    part_send_sem,
    part_recv_sem,
    table_send_sem,
    table_recv_sem,
    send_sem,
    recv_sem,
):
    me = lax.axis_index("band")
    nodes_dev, width = mesh_embed.shape
    layers = edge_w1.shape[0]
    cap = fetch_table.shape[2]
    edge_rows = edge_latent.shape[0]
    grid_rows = grid_feats.shape[1]

    peers = peer_order(me, n)
    barrier = pltpu.get_barrier_semaphore()
    for peer in peers:
        pl.semaphore_signal(barrier, inc=1, device_id={"band": peer})

    pairs = [
        (grid_node, gn),
        (w_grid, wg),
        (grid_feats, gf),
        (fetch_table.at[0], table),
        (edge_sender, es),
        (edge_receiver, er),
        (block_count, count),
        (mesh_embed, me_v),
        (enc_w1, ew1),
        (enc_w2, ew2),
        (edge_w1, e1),
        (edge_latent, edges),
        (node_w2, n2),
        (edge_w2, e2),
        (node_w1, n1),
    ]
    loads = [
        pltpu.make_async_copy(source, target, load_sem.at[index])
        for index, (source, target) in enumerate(pairs)
    ]
    for load in loads[:7]:
        load.start()

    loads[0].wait()
    first = (me - 1) * nodes_dev
    for row in range(grid_rows // LANES):
        column = gn[row : row + 1, :] - first
        hot = lax.broadcasted_iota(jnp.int32, (3 * nodes_dev, LANES), 0) == column
        grid_hot[:, row * LANES : (row + 1) * LANES] = hot.astype(F32).astype(BF16)
    loads[3].wait()
    for owner in range(n):
        table_send[owner, :, :cap] = table[owner : owner + 1, :]
    table_recv[n - 1] = table_send[me]
    loads[1].wait()
    wg_t[...] = wg[...].T
    loads[2].wait()
    for load in loads[7:]:
        load.start()
    for start in range(0, grid_rows, ROWS):
        rows = slice(start, start + ROWS)
        latent[:, rows] = silu(dot(wg_t[...], gf[:, rows])).astype(BF16)
    partial = lax.dot_general(
        grid_hot[...], latent[...], (((1,), (1,)), ((), ())), preferred_element_type=F32
    )
    part_send[0] = partial[:nodes_dev].astype(BF16)
    part_send[1] = partial[2 * nodes_dev :].astype(BF16)
    own = partial[nodes_dev : 2 * nodes_dev]

    pl.semaphore_wait(barrier, n - 1)

    def part_copy(slot, target):
        return pltpu.make_async_remote_copy(
            src_ref=part_send.at[slot],
            dst_ref=part_recv.at[slot],
            send_sem=part_send_sem.at[slot],
            recv_sem=part_recv_sem.at[slot],
            device_id={"band": target},
        )

    below = lax.rem(me + n - 1, n)
    above = lax.rem(me + 1, n)
    down = part_copy(0, below)
    up = part_copy(1, above)

    def table_copy(slot, peer):
        return pltpu.make_async_remote_copy(
            src_ref=table_send.at[peer],
            dst_ref=table_recv.at[slot],
            send_sem=table_send_sem,
            recv_sem=table_recv_sem,
            device_id={"band": peer},
        )

    half = n // 2
    for slot in range(half):
        table_copy(slot, peers[slot]).start()

    @pl.when(me > 0)
    def _():
        down.start()

    @pl.when(me < n - 1)
    def _():
        up.start()

    for slot in range(half, n - 1):
        table_copy(slot, peers[slot]).start()

    loads[4].wait()
    loads[5].wait()
    loads[6].wait()
    live_rows = count[0] * EDGE_BLOCK
    slots = es[...]
    owner = lax.div(slots, cap)
    slots = slot_of(owner, peers) * cap + (slots - owner * cap)
    for row in range(edge_rows // LANES):
        rows = slice(row * LANES, (row + 1) * LANES)
        lane = lax.broadcasted_iota(jnp.int32, (LANES, LANES), 1)
        sender = jnp.broadcast_to(slots[row : row + 1, :], (LANES, LANES)).T
        for base in range(0, n * cap, LANES):
            hot = (sender == lane + base).astype(F32).astype(BF16)
            send_hot[rows, base : base + LANES] = hot
        value = er[row : row + 1, :]
        receiver = jnp.broadcast_to(value, (LANES, LANES)).T
        for base in range(0, nodes_dev, LANES):
            hot = (receiver == lane + base).astype(F32).astype(BF16)
            recv_hot[rows, base : base + LANES] = hot
        place = lax.broadcasted_iota(jnp.int32, (1, LANES), 1) + row * LANES
        masked = jnp.where(place < live_rows, value, -1)
        hot = lax.broadcasted_iota(jnp.int32, (nodes_dev, LANES), 0) == masked
        recv_hot_t[:, rows] = hot.astype(F32).astype(BF16)

    def sender_weight(layer):
        return e1[layer, width : 2 * width, :]

    for index in range(7, 15):
        loads[index].wait()
    ew2[...] = center(ew2[...])
    mixed[layers - 1] = dot(ew2[...], sender_weight(0)).astype(BF16)
    embed_sent = dot(me_v[...], sender_weight(0)) * 0.5
    for layer in range(layers):
        e2[layer] = center(e2[layer])
        n2[layer] = center(n2[layer])
        joint[layer] = dot(e2[layer], n1[layer, width:, :]).astype(BF16)
    for layer in range(layers - 1):
        mixed[layer] = dot(n2[layer], sender_weight(layer + 1)).astype(BF16)

    @pl.when(me > 0)
    def _():
        part_copy(1, above).wait_recv()

    @pl.when(me == 0)
    def _():
        part_recv[1] = jnp.zeros((nodes_dev, width), BF16)

    @pl.when(me < n - 1)
    def _():
        part_copy(0, below).wait_recv()

    @pl.when(me == n - 1)
    def _():
        part_recv[0] = jnp.zeros((nodes_dev, width), BF16)

    agg = own + part_recv[0].astype(F32) + part_recv[1].astype(F32)
    hidden = silu(dot(agg.astype(BF16), ew1[...])).astype(BF16)
    update = dot(hidden, ew2[...])
    turned = dot(hidden, mixed[layers - 1])
    scale = inverse_scale(update)
    sent = (embed_sent + (0.5 * scale) * turned).astype(BF16)
    nodes_ref[...] = (me_v[...].astype(F32) + scale * update).astype(BF16)

    def several(refs, sems):
        return pltpu.make_async_copy(refs, refs, sems)

    several(table_recv.at[pl.ds(0, n - 1)], table_recv_sem).wait()
    def choose(first, size):
        rows = slice(first * cap, (first + size) * cap)
        wanted = jnp.broadcast_to(table_recv[first : first + size], (size, cap, LANES))
        wanted = wanted.reshape(size * cap, LANES)
        slot = lax.rem(lax.broadcasted_iota(jnp.int32, (size * cap, LANES), 0), cap)
        lane = lax.broadcasted_iota(jnp.int32, (size * cap, LANES), 1)
        column = jnp.sum(jnp.where(slot == lane, wanted, 0).astype(F32), axis=1, keepdims=True)
        lane = lax.broadcasted_iota(jnp.int32, (size * cap, nodes_dev), 1).astype(F32)
        pick[rows, :] = (column == lane).astype(F32).astype(BF16)
        chosen = dot(pick[rows, :], sent).astype(BF16)
        outgoing[first : first + size] = chosen.reshape(size, cap, width)

    def layer_copy(layer, slot, peer):
        return pltpu.make_async_remote_copy(
            src_ref=outgoing.at[slot],
            dst_ref=incoming.at[lax.rem(layer, 2), slot],
            send_sem=send_sem,
            recv_sem=recv_sem.at[lax.rem(layer, 2)],
            device_id={"band": peer},
        )

    def send(layer, slots):
        for slot in slots:
            layer_copy(layer, slot, peers[slot]).start()

    def keep(layer):
        incoming[lax.rem(layer, 2), n - 1] = outgoing[n - 1]

    def prepare(layer):
        nodes = nodes_ref[...]
        kept = dot(nodes, e1[layer, 2 * width :, :]).astype(BF16)
        for start in range(0, edge_rows, ROWS):
            rows = slice(start, start + ROWS)
            joined = dot(edges[rows, :], e1[layer, :width, :]) + dot(recv_hot[rows, :], kept)
            local[rows, :] = joined * 0.5

    def prepare_picked(layer):
        base = dot(pick_sum[...], edges[...]).astype(BF16)
        part = dot(picked[...], n1[layer, :width, :])
        picked_part[...] = part + dot(base, n1[layer, width:, :])
        picked_sent[...] = dot(picked[...], sender_weight(layer + 1)) * 0.5

    def arrivals(layer):
        parity = lax.rem(layer, 2)
        several(outgoing.at[pl.ds(0, n - 1)], send_sem).wait()
        several(incoming.at[parity, pl.ds(0, n - 1)], recv_sem.at[parity]).wait()
        senders = incoming[parity].reshape(n * cap, width)
        pieces = [slice(start, start + CHUNK) for start in range(0, edge_rows, CHUNK)]
        hiddens = {}
        values = {}
        turned = {}
        for step in range(len(pieces) + 2):
            if step < len(pieces):
                rows = pieces[step]
                before = local[rows, :] + dot(send_hot[rows, :], senders)
                hiddens[step] = silu_of_half(before.astype(BF16))
            if 0 <= step - 1 < len(pieces):
                values[step - 1] = dot(hiddens[step - 1], e2[layer])
                turned[step - 1] = dot(hiddens[step - 1], joint[layer])
            if 0 <= step - 2:
                rows = pieces[step - 2]
                value = values[step - 2]
                message[rows, :] = value.astype(BF16)
                turned_message[rows, :] = (turned[step - 2] * inverse_scale(value)).astype(BF16)

    groups = ((0, half), (half, n - half))
    for first, size in groups:
        choose(first, size)
        send(0, range(first, min(first + size, n - 1)))
    keep(0)
    pick_sum[...] = dot(pick[...], recv_hot_t[...]).astype(BF16)
    picked[...] = dot(pick[...], nodes_ref[...]).astype(BF16)
    prepare(0)
    if layers > 1:
        prepare_picked(0)

    def run_layer(layer, carry):
        arrivals(layer)
        for first, size in groups:
            rows = slice(first * cap, (first + size) * cap)
            before = picked_part[rows, :] + dot(pick_sum[rows, :], turned_message[...])
            hidden = silu(before).astype(BF16)
            update = dot(hidden, n2[layer])
            turned = dot(hidden, mixed[layer])
            scale = inverse_scale(update)
            sent = picked_sent[rows, :] + (0.5 * scale) * turned
            outgoing[first : first + size] = sent.astype(BF16).reshape(size, cap, width)
            send(layer + 1, range(first, min(first + size, n - 1)))
            picked[rows, :] = (picked[rows, :].astype(F32) + scale * update).astype(BF16)
        keep(layer + 1)
        for start in range(0, edge_rows, ROWS):
            rows = slice(start, start + ROWS)
            value = message[rows, :].astype(F32)
            value = value * inverse_scale(value)
            edges[rows, :] = (edges[rows, :].astype(F32) + value).astype(BF16)
        summed = dot(recv_hot_t[...], edges[...]).astype(BF16)
        nodes = nodes_ref[...]
        before = dot(nodes, n1[layer, :width, :]) + dot(summed, n1[layer, width:, :])
        update = dot(silu(before).astype(BF16), n2[layer])
        nodes_ref[...] = (nodes.astype(F32) + update * inverse_scale(update)).astype(BF16)
        prepare(layer + 1)
        prepare_picked(lax.min(layer + 1, layers - 2))
        return carry

    lax.fori_loop(0, layers - 1, run_layer, 0)

    last = layers - 1
    nodes = nodes_ref[...]
    base = dot(recv_hot_t[...], edges[...]).astype(BF16)
    part = dot(nodes, n1[last, :width, :]) + dot(base, n1[last, width:, :])
    arrivals(last)
    hidden = silu(part + dot(recv_hot_t[...], turned_message[...])).astype(BF16)
    update = dot(hidden, n2[last])
    out[...] = (nodes.astype(F32) + update * inverse_scale(update)).astype(BF16)

    several(table_send.at[pl.ds(0, n - 1)], table_send_sem).wait()

    @pl.when(me > 0)
    def _():
        part_copy(0, below).wait_send()

    @pl.when(me < n - 1)
    def _():
        part_copy(1, above).wait_send()


def shards(n, *args):
    grid_feats, mesh_embed, edge_latent = args[:3]
    grid_node, fetch_table, edge_sender, edge_receiver, block_count = args[3:8]
    weights = args[8:]
    grid_node = grid_node.reshape(-1, LANES)
    edge_sender = edge_sender.reshape(-1, LANES)
    edge_receiver = edge_receiver.reshape(-1, LANES)
    grid_feats = grid_feats.T
    grid_rows = grid_feats.shape[1]
    edge_rows = edge_latent.shape[0]
    nodes_dev, width = mesh_embed.shape
    cap = fetch_table.shape[2]
    layers = weights[3].shape[0]
    anywhere = pl.BlockSpec(memory_space=pltpu.HBM)

    def like(array):
        return pltpu.VMEM(array.shape, array.dtype)

    return pl.pallas_call(
        functools.partial(kernel, n),
        out_shape=pltpu.VMEM(mesh_embed.shape, mesh_embed.dtype),
        in_specs=[anywhere] * 15,
        out_specs=pl.BlockSpec(memory_space=pltpu.VMEM),
        scratch_shapes=[
            like(grid_feats),
            like(weights[0]),
            pltpu.VMEM(weights[0].shape[::-1], BF16),
            like(mesh_embed),
            *[like(weight) for weight in weights[1:]],
            like(edge_latent),
            like(grid_node),
            pltpu.VMEM(fetch_table.shape[1:], jnp.int32),
            like(edge_sender),
            like(edge_receiver),
            pltpu.SMEM(block_count.shape, block_count.dtype),
            pltpu.VMEM((3 * nodes_dev, grid_rows), BF16),
            pltpu.VMEM((width, grid_rows), BF16),
            pltpu.VMEM((2, nodes_dev, width), BF16),
            pltpu.VMEM((2, nodes_dev, width), BF16),
            pltpu.VMEM((n, 1, LANES), jnp.int32),
            pltpu.VMEM((n, 1, LANES), jnp.int32),
            pltpu.VMEM((n * cap, nodes_dev), BF16),
            pltpu.VMEM((n * cap, edge_rows), BF16),
            pltpu.VMEM((edge_rows, n * cap), BF16),
            pltpu.VMEM((edge_rows, nodes_dev), BF16),
            pltpu.VMEM((nodes_dev, edge_rows), BF16),
            pltpu.VMEM((edge_rows, width), F32),
            pltpu.VMEM((edge_rows, width), BF16),
            pltpu.VMEM((edge_rows, width), BF16),
            pltpu.VMEM((nodes_dev, width), BF16),
            pltpu.VMEM((n * cap, width), BF16),
            pltpu.VMEM((n * cap, width), F32),
            pltpu.VMEM((n * cap, width), F32),
            pltpu.VMEM((layers, width, width), BF16),
            pltpu.VMEM((layers, width, width), BF16),
            pltpu.VMEM((n, cap, width), BF16),
            pltpu.VMEM((2, n, cap, width), BF16),
            pltpu.SemaphoreType.DMA((15,)),
            pltpu.SemaphoreType.DMA((2,)),
            pltpu.SemaphoreType.DMA((2,)),
            pltpu.SemaphoreType.DMA,
            pltpu.SemaphoreType.DMA,
            pltpu.SemaphoreType.DMA,
            pltpu.SemaphoreType.DMA((2,)),
        ],
        compiler_params=pltpu.CompilerParams(
            collective_id=0, has_side_effects=True, vmem_limit_bytes=66_900_000
        ),
        name="graph_net",
    )(
        grid_feats,
        mesh_embed,
        edge_latent,
        grid_node,
        fetch_table,
        edge_sender,
        edge_receiver,
        block_count,
        *weights,
    )


def solution(mesh):
    return jax.shard_map(
        functools.partial(shards, mesh.shape["band"]),
        mesh=mesh,
        in_specs=(
            P(("groups", "band"), None),
            P(("groups", "band"), None),
            P(("groups", "band"), None),
            P("band"),
            P("band", None, None),
            P("band"),
            P("band"),
            P("band"),
            P(),
            P(),
            P(),
            P(),
            P(),
            P(),
            P(),
        ),
        out_specs=P(("groups", "band"), None),
        check_vma=False,
    )
```

```python
import functools

import jax
import jax.numpy as jnp
from jax import lax
from jax.experimental import pallas as pl
from jax.experimental.pallas import tpu as pltpu
from jax.sharding import PartitionSpec as P

EDGE_BLOCK = 128
LANES = 128
ROWS = 256
CHUNK = 512
F32 = jnp.float32
BF16 = jnp.bfloat16


def silu_of_half(half):
    return half + half * jnp.tanh(half)


def silu(value):
    return silu_of_half(value * 0.5)


def center(weight):
    value = weight.astype(F32)
    return (value - jnp.mean(value, axis=-1, keepdims=True)).astype(BF16)


def inverse_scale(value):
    var = jnp.sum(value * value, axis=-1, keepdims=True) * (1.0 / value.shape[-1])
    return lax.rsqrt(var + 1e-05)


def dot(left, right):
    return jnp.dot(left, right, preferred_element_type=F32)


def flipped(me, bits):
    place, result = 1, 0
    while place <= bits or place == 1:
        bit = lax.rem(lax.div(me, place), 2)
        result += place * ((1 - bit if bits & place else bit) - bit)
        place *= 2
    return me + result


def peer_order(me, n):
    assert n & (n - 1) == 0
    return [flipped(me, bits) for bits in sorted(range(1, n), key=lambda bits: (-(bits >= n // 2), bits & 1, -bits))]


def slot_of(owner, peers):
    slot = jnp.full(owner.shape, len(peers), jnp.int32)
    for place, peer in enumerate(peers):
        slot = jnp.where(owner == peer, place, slot)
    return slot


def kernel(
    n,
    grid_feats,
    mesh_embed,
    edge_latent,
    grid_node,
    fetch_table,
    edge_sender,
    edge_receiver,
    block_count,
    w_grid,
    enc_w1,
    enc_w2,
    edge_w1,
    edge_w2,
    node_w1,
    node_w2,
    out,
    gf,
    wg,
    wg_t,
    me_v,
    ew1,
    ew2,
    e1,
    e2,
    n1,
    n2,
    edges,
    gn,
    table,
    es,
    er,
    count,
    grid_hot,
    latent,
    part_send,
    part_recv,
    table_send,
    table_recv,
    pick,
    pick_sum,
    send_hot,
    recv_hot,
    recv_hot_t,
    local,
    message,
    turned_message,
    nodes_ref,
    picked,
    picked_part,
    picked_sent,
    mixed,
    joint,
    outgoing,
    incoming,
    load_sem,
    part_send_sem,
    part_recv_sem,
    table_send_sem,
    table_recv_sem,
    send_sem,
    recv_sem,
):
    me = lax.axis_index("band")
    nodes_dev, width = mesh_embed.shape
    layers = edge_w1.shape[0]
    cap = fetch_table.shape[2]
    edge_rows = edge_latent.shape[0]
    grid_rows = grid_feats.shape[1]

    peers = peer_order(me, n)
    barrier = pltpu.get_barrier_semaphore()
    for peer in peers:
        pl.semaphore_signal(barrier, inc=1, device_id={"band": peer})

    pairs = [
        (grid_node, gn),
        (w_grid, wg),
        (grid_feats, gf),
        (fetch_table.at[0], table),
        (edge_sender, es),
        (edge_receiver, er),
        (block_count, count),
        (mesh_embed, me_v),
        (enc_w1, ew1),
        (enc_w2, ew2),
        (edge_w1, e1),
        (edge_latent, edges),
        (node_w2, n2),
        (edge_w2, e2),
        (node_w1, n1),
    ]
    loads = [
        pltpu.make_async_copy(source, target, load_sem.at[index])
        for index, (source, target) in enumerate(pairs)
    ]
    for load in loads[:7]:
        load.start()

    loads[0].wait()
    first = (me - 1) * nodes_dev
    for row in range(grid_rows // LANES):
        column = gn[row : row + 1, :] - first
        hot = lax.broadcasted_iota(jnp.int32, (3 * nodes_dev, LANES), 0) == column
        grid_hot[:, row * LANES : (row + 1) * LANES] = hot.astype(F32).astype(BF16)
    loads[3].wait()
    for owner in range(n):
        table_send[owner, :, :cap] = table[owner : owner + 1, :]
    table_recv[n - 1] = table_send[me]
    loads[1].wait()
    wg_t[...] = wg[...].T
    loads[2].wait()
    for load in loads[7:]:
        load.start()
    for start in range(0, grid_rows, ROWS):
        rows = slice(start, start + ROWS)
        latent[:, rows] = silu(dot(wg_t[...], gf[:, rows])).astype(BF16)
    partial = lax.dot_general(
        grid_hot[...], latent[...], (((1,), (1,)), ((), ())), preferred_element_type=F32
    )
    part_send[0] = partial[:nodes_dev].astype(BF16)
    part_send[1] = partial[2 * nodes_dev :].astype(BF16)
    own = partial[nodes_dev : 2 * nodes_dev]

    pl.semaphore_wait(barrier, n - 1)

    def part_copy(slot, target):
        return pltpu.make_async_remote_copy(
            src_ref=part_send.at[slot],
            dst_ref=part_recv.at[slot],
            send_sem=part_send_sem.at[slot],
            recv_sem=part_recv_sem.at[slot],
            device_id={"band": target},
        )

    below = lax.rem(me + n - 1, n)
    above = lax.rem(me + 1, n)
    down = part_copy(0, below)
    up = part_copy(1, above)

    def table_copy(slot, peer):
        return pltpu.make_async_remote_copy(
            src_ref=table_send.at[peer],
            dst_ref=table_recv.at[slot],
            send_sem=table_send_sem,
            recv_sem=table_recv_sem,
            device_id={"band": peer},
        )

    half = n // 2
    for slot in range(half):
        table_copy(slot, peers[slot]).start()

    @pl.when(me > 0)
    def _():
        down.start()

    @pl.when(me < n - 1)
    def _():
        up.start()

    for slot in range(half, n - 1):
        table_copy(slot, peers[slot]).start()

    loads[4].wait()
    loads[5].wait()
    loads[6].wait()
    live_rows = count[0] * EDGE_BLOCK
    slots = es[...]
    owner = lax.div(slots, cap)
    slots = slot_of(owner, peers) * cap + (slots - owner * cap)
    for row in range(edge_rows // LANES):
        rows = slice(row * LANES, (row + 1) * LANES)
        lane = lax.broadcasted_iota(jnp.int32, (LANES, LANES), 1)
        sender = jnp.broadcast_to(slots[row : row + 1, :], (LANES, LANES)).T
        for base in range(0, n * cap, LANES):
            hot = (sender == lane + base).astype(F32).astype(BF16)
            send_hot[rows, base : base + LANES] = hot
        value = er[row : row + 1, :]
        receiver = jnp.broadcast_to(value, (LANES, LANES)).T
        for base in range(0, nodes_dev, LANES):
            hot = (receiver == lane + base).astype(F32).astype(BF16)
            recv_hot[rows, base : base + LANES] = hot
        place = lax.broadcasted_iota(jnp.int32, (1, LANES), 1) + row * LANES
        masked = jnp.where(place < live_rows, value, -1)
        hot = lax.broadcasted_iota(jnp.int32, (nodes_dev, LANES), 0) == masked
        recv_hot_t[:, rows] = hot.astype(F32).astype(BF16)

    def sender_weight(layer):
        return e1[layer, width : 2 * width, :]

    for index in range(7, 15):
        loads[index].wait()
    ew2[...] = center(ew2[...])
    mixed[layers - 1] = dot(ew2[...], sender_weight(0)).astype(BF16)
    embed_sent = dot(me_v[...], sender_weight(0)) * 0.5
    for layer in range(layers):
        e2[layer] = center(e2[layer])
        n2[layer] = center(n2[layer])
        joint[layer] = dot(e2[layer], n1[layer, width:, :]).astype(BF16)
    for layer in range(layers - 1):
        mixed[layer] = dot(n2[layer], sender_weight(layer + 1)).astype(BF16)

    @pl.when(me > 0)
    def _():
        part_copy(1, above).wait_recv()

    @pl.when(me == 0)
    def _():
        part_recv[1] = jnp.zeros((nodes_dev, width), BF16)

    @pl.when(me < n - 1)
    def _():
        part_copy(0, below).wait_recv()

    @pl.when(me == n - 1)
    def _():
        part_recv[0] = jnp.zeros((nodes_dev, width), BF16)

    agg = own + part_recv[0].astype(F32) + part_recv[1].astype(F32)
    hidden = silu(dot(agg.astype(BF16), ew1[...])).astype(BF16)
    update = dot(hidden, ew2[...])
    turned = dot(hidden, mixed[layers - 1])
    scale = inverse_scale(update)
    sent = (embed_sent + (0.5 * scale) * turned).astype(BF16)
    nodes_ref[...] = (me_v[...].astype(F32) + scale * update).astype(BF16)

    def several(refs, sems):
        return pltpu.make_async_copy(refs, refs, sems)

    several(table_recv.at[pl.ds(0, n - 1)], table_recv_sem).wait()
    def choose(first, size):
        rows = slice(first * cap, (first + size) * cap)
        wanted = jnp.broadcast_to(table_recv[first : first + size], (size, cap, LANES))
        wanted = wanted.reshape(size * cap, LANES)
        slot = lax.rem(lax.broadcasted_iota(jnp.int32, (size * cap, LANES), 0), cap)
        lane = lax.broadcasted_iota(jnp.int32, (size * cap, LANES), 1)
        column = jnp.sum(jnp.where(slot == lane, wanted, 0).astype(F32), axis=1, keepdims=True)
        lane = lax.broadcasted_iota(jnp.int32, (size * cap, nodes_dev), 1).astype(F32)
        pick[rows, :] = (column == lane).astype(F32).astype(BF16)
        chosen = dot(pick[rows, :], sent).astype(BF16)
        outgoing[first : first + size] = chosen.reshape(size, cap, width)

    def layer_copy(layer, slot, peer):
        return pltpu.make_async_remote_copy(
            src_ref=outgoing.at[slot],
            dst_ref=incoming.at[lax.rem(layer, 2), slot],
            send_sem=send_sem,
            recv_sem=recv_sem.at[lax.rem(layer, 2)],
            device_id={"band": peer},
        )

    def send(layer, slots):
        for slot in slots:
            layer_copy(layer, slot, peers[slot]).start()

    def keep(layer):
        incoming[lax.rem(layer, 2), n - 1] = outgoing[n - 1]

    def prepare(layer):
        nodes = nodes_ref[...]
        kept = dot(nodes, e1[layer, 2 * width :, :]).astype(BF16)
        for start in range(0, edge_rows, ROWS):
            rows = slice(start, start + ROWS)
            joined = dot(edges[rows, :], e1[layer, :width, :]) + dot(recv_hot[rows, :], kept)
            local[rows, :] = joined * 0.5

    def prepare_picked(layer):
        base = dot(pick_sum[...], edges[...]).astype(BF16)
        part = dot(picked[...], n1[layer, :width, :])
        picked_part[...] = part + dot(base, n1[layer, width:, :])
        picked_sent[...] = dot(picked[...], sender_weight(layer + 1)) * 0.5

    def arrivals(layer):
        parity = lax.rem(layer, 2)
        several(outgoing.at[pl.ds(0, n - 1)], send_sem).wait()
        several(incoming.at[parity, pl.ds(0, n - 1)], recv_sem.at[parity]).wait()
        senders = incoming[parity].reshape(n * cap, width)
        pieces = [slice(start, start + CHUNK) for start in range(0, edge_rows, CHUNK)]
        hiddens = {}
        values = {}
        turned = {}
        for step in range(len(pieces) + 2):
            if step < len(pieces):
                rows = pieces[step]
                before = local[rows, :] + dot(send_hot[rows, :], senders)
                hiddens[step] = silu_of_half(before.astype(BF16))
            if 0 <= step - 1 < len(pieces):
                values[step - 1] = dot(hiddens[step - 1], e2[layer])
                turned[step - 1] = dot(hiddens[step - 1], joint[layer])
            if 0 <= step - 2:
                rows = pieces[step - 2]
                value = values[step - 2]
                message[rows, :] = value.astype(BF16)
                turned_message[rows, :] = (turned[step - 2] * inverse_scale(value)).astype(BF16)

    groups = ((0, half), (half, n - half))
    for first, size in groups:
        choose(first, size)
        send(0, range(first, min(first + size, n - 1)))
    keep(0)
    pick_sum[...] = dot(pick[...], recv_hot_t[...]).astype(BF16)
    picked[...] = dot(pick[...], nodes_ref[...]).astype(BF16)
    prepare(0)
    if layers > 1:
        prepare_picked(0)

    def run_layer(layer, carry):
        arrivals(layer)
        for first, size in groups:
            rows = slice(first * cap, (first + size) * cap)
            before = picked_part[rows, :] + dot(pick_sum[rows, :], turned_message[...])
            hidden = silu(before).astype(BF16)
            update = dot(hidden, n2[layer])
            turned = dot(hidden, mixed[layer])
            scale = inverse_scale(update)
            sent = picked_sent[rows, :] + (0.5 * scale) * turned
            outgoing[first : first + size] = sent.astype(BF16).reshape(size, cap, width)
            send(layer + 1, range(first, min(first + size, n - 1)))
            picked[rows, :] = (picked[rows, :].astype(F32) + scale * update).astype(BF16)
        keep(layer + 1)
        for start in range(0, edge_rows, ROWS):
            rows = slice(start, start + ROWS)
            value = message[rows, :].astype(F32)
            value = value * inverse_scale(value)
            edges[rows, :] = (edges[rows, :].astype(F32) + value).astype(BF16)
        summed = dot(recv_hot_t[...], edges[...]).astype(BF16)
        nodes = nodes_ref[...]
        before = dot(nodes, n1[layer, :width, :]) + dot(summed, n1[layer, width:, :])
        update = dot(silu(before).astype(BF16), n2[layer])
        nodes_ref[...] = (nodes.astype(F32) + update * inverse_scale(update)).astype(BF16)
        prepare(layer + 1)

        @pl.when(layer < layers - 2)
        def _():
            prepare_picked(layer + 1)

        return carry

    lax.fori_loop(0, layers - 1, run_layer, 0)

    last = layers - 1
    nodes = nodes_ref[...]
    base = dot(recv_hot_t[...], edges[...]).astype(BF16)
    part = dot(nodes, n1[last, :width, :]) + dot(base, n1[last, width:, :])
    arrivals(last)
    hidden = silu(part + dot(recv_hot_t[...], turned_message[...])).astype(BF16)
    update = dot(hidden, n2[last])
    out[...] = (nodes.astype(F32) + update * inverse_scale(update)).astype(BF16)

    several(table_send.at[pl.ds(0, n - 1)], table_send_sem).wait()

    @pl.when(me > 0)
    def _():
        part_copy(0, below).wait_send()

    @pl.when(me < n - 1)
    def _():
        part_copy(1, above).wait_send()


def shards(n, *args):
    grid_feats, mesh_embed, edge_latent = args[:3]
    grid_node, fetch_table, edge_sender, edge_receiver, block_count = args[3:8]
    weights = args[8:]
    grid_node = grid_node.reshape(-1, LANES)
    edge_sender = edge_sender.reshape(-1, LANES)
    edge_receiver = edge_receiver.reshape(-1, LANES)
    grid_feats = grid_feats.T
    grid_rows = grid_feats.shape[1]
    edge_rows = edge_latent.shape[0]
    nodes_dev, width = mesh_embed.shape
    cap = fetch_table.shape[2]
    layers = weights[3].shape[0]
    anywhere = pl.BlockSpec(memory_space=pltpu.HBM)

    def like(array):
        return pltpu.VMEM(array.shape, array.dtype)

    return pl.pallas_call(
        functools.partial(kernel, n),
        out_shape=pltpu.VMEM(mesh_embed.shape, mesh_embed.dtype),
        in_specs=[anywhere] * 15,
        out_specs=pl.BlockSpec(memory_space=pltpu.VMEM),
        scratch_shapes=[
            like(grid_feats),
            like(weights[0]),
            pltpu.VMEM(weights[0].shape[::-1], BF16),
            like(mesh_embed),
            *[like(weight) for weight in weights[1:]],
            like(edge_latent),
            like(grid_node),
            pltpu.VMEM(fetch_table.shape[1:], jnp.int32),
            like(edge_sender),
            like(edge_receiver),
            pltpu.SMEM(block_count.shape, block_count.dtype),
            pltpu.VMEM((3 * nodes_dev, grid_rows), BF16),
            pltpu.VMEM((width, grid_rows), BF16),
            pltpu.VMEM((2, nodes_dev, width), BF16),
            pltpu.VMEM((2, nodes_dev, width), BF16),
            pltpu.VMEM((n, 1, LANES), jnp.int32),
            pltpu.VMEM((n, 1, LANES), jnp.int32),
            pltpu.VMEM((n * cap, nodes_dev), BF16),
            pltpu.VMEM((n * cap, edge_rows), BF16),
            pltpu.VMEM((edge_rows, n * cap), BF16),
            pltpu.VMEM((edge_rows, nodes_dev), BF16),
            pltpu.VMEM((nodes_dev, edge_rows), BF16),
            pltpu.VMEM((edge_rows, width), F32),
            pltpu.VMEM((edge_rows, width), BF16),
            pltpu.VMEM((edge_rows, width), BF16),
            pltpu.VMEM((nodes_dev, width), BF16),
            pltpu.VMEM((n * cap, width), BF16),
            pltpu.VMEM((n * cap, width), F32),
            pltpu.VMEM((n * cap, width), F32),
            pltpu.VMEM((layers, width, width), BF16),
            pltpu.VMEM((layers, width, width), BF16),
            pltpu.VMEM((n, cap, width), BF16),
            pltpu.VMEM((2, n, cap, width), BF16),
            pltpu.SemaphoreType.DMA((15,)),
            pltpu.SemaphoreType.DMA((2,)),
            pltpu.SemaphoreType.DMA((2,)),
            pltpu.SemaphoreType.DMA,
            pltpu.SemaphoreType.DMA,
            pltpu.SemaphoreType.DMA,
            pltpu.SemaphoreType.DMA((2,)),
        ],
        compiler_params=pltpu.CompilerParams(
            collective_id=0, has_side_effects=True, vmem_limit_bytes=66_900_000
        ),
        name="graph_net",
    )(
        grid_feats,
        mesh_embed,
        edge_latent,
        grid_node,
        fetch_table,
        edge_sender,
        edge_receiver,
        block_count,
        *weights,
    )


def solution(mesh):
    return jax.shard_map(
        functools.partial(shards, mesh.shape["band"]),
        mesh=mesh,
        in_specs=(
            P(("groups", "band"), None),
            P(("groups", "band"), None),
            P(("groups", "band"), None),
            P("band"),
            P("band", None, None),
            P("band"),
            P("band"),
            P("band"),
            P(),
            P(),
            P(),
            P(),
            P(),
            P(),
            P(),
        ),
        out_specs=P(("groups", "band"), None),
        check_vma=False,
    )
```
